256 devices in a mesh: dp: 32 (over y, x, core), expert: 8 (over z).
Axes of the slice: x: 4, y: 4, z: 8, core: 2. Of those that a mesh axis runs over, the one named last changes fastest.
Arguments:
- tokens: bfloat16 [4096, 2048], P('dp'), may hold values from -6 to 6
- route_expert: int32 [4096, 4], P('dp'), may hold values from 0 to 31, all different within a row; in each aligned block of 128 rows (0 to 127, 128 to 255, ...) at most 32 rows name the same one
- route_weight: float32 [4096, 4], P('dp'), may hold values from 0.1 to 1
- gate_weight: bfloat16 [32, 1408, 2048], P('dp', 'expert'), may hold values from -0.125 to 0.125
- up_weight: bfloat16 [32, 1408, 2048], P('dp', 'expert'), may hold values from -0.125 to 0.125
- down_weight: bfloat16 [32, 1408, 2048], P('dp', 'expert'), may hold values from -0.15625 to 0.15625
- gate_scale: float32 [32, 1408], P('dp', 'expert'), may hold values from 0.5 to 2
- up_scale: float32 [32, 1408], P('dp', 'expert'), may hold values from 0.5 to 2
- down_scale: float32 [32, 2048], replicated, may hold values from 0.5 to 2
- cotangent: bfloat16 [4096, 2048], P('dp', 'expert'), may hold values from -6 to 6
Outputs:
- mixed: bfloat16 [4096, 2048], P('dp', 'expert')
- token_grad: bfloat16 [4096, 2048], P('dp', 'expert')
- route_grad: float32 [4096, 4], P('dp')
- gate_grad: float32 [32, 1408, 2048], P('dp', 'expert')
- up_grad: float32 [32, 1408, 2048], P('dp', 'expert')
- down_grad: float32 [32, 1408, 2048], P('dp', 'expert')
The draws below stay inside these ranges and needn't reach their ends.
Inputs may be any that keep to these rules, and one draw needn't show every extreme that they name: `route_expert`: each row names 4 different experts. Among the 128 rows of one aligned block (the tokens of one index of dp) no expert is named by more than 32 rows, and in some block one expert is named by exactly 32 rows.
All inputs are finite; a program needn't handle non-finite values.
Results may differ from the reference program's by a relative error of at most 0.0058.
Values may be sent and summed in bfloat16 or wider, within the bound.
No kernel may reach another device: no remote copies, remote signals or barrier semaphores. Data moves between devices by JAX's collectives and lax.ppermute only.
A program may use at most 128 MiB of HBM per device.

```python
import math
import jax
import jax.numpy as jnp
import numpy as np
from jax import lax

D = 2048
FF = 1408
TOP = 4
TOK_DEV = 128
EXPERTS = 32
TOKENS = 4096
CAP = 32
N_DP = 32


def block_levels(own_key, shape, split, low, high):
    loudness = 1.0
    for dim, parts in split:
        heights = jax.random.uniform(jax.random.fold_in(jax.random.fold_in(own_key, 6), dim), (parts,), jnp.float32, low / len(split), high / len(split))
        loudness = loudness * jnp.repeat(jnp.exp(heights), shape[dim] // parts).reshape((-1,) + (1,) * (len(shape) - 1 - dim))
    return loudness


def deal_out(stream_key, own, number, rows, amount, top, limit, skew):
    sequence = jax.random.permutation(stream_key, amount)
    crowded, common = load_shares(amount, rows * top, limit, skew, True), load_shares(amount, rows * top, limit, skew, False)
    places = jnp.arange(amount)

    def named(tallies, offset_by):
        used = int((tallies > 0).sum())
        fixed = max(1, used // 4)
        moved = fixed + (places - fixed + offset_by * (used - fixed)) % max(1, amount - fixed)
        return jnp.zeros((amount,), jnp.int32).at[sequence[jnp.where(places < fixed, places, moved)]].set(jnp.asarray(tallies, jnp.int32))

    tallies = jnp.where(number % 4 == 0, named(crowded, number // 4), named(common, number - number // 4 - 1))
    mixed = jax.random.permutation(jax.random.fold_in(own, 3), amount)
    source_of, taker = mixed[0:amount // 2 * 2:2], mixed[1:amount // 2 * 2:2]
    margin = jnp.minimum(tallies[source_of] - 1, limit - tallies[taker]) // 2
    margin = jnp.where((source_of == sequence[0]) | (taker == sequence[0]) | (tallies[taker] == 0), 0, jnp.maximum(margin, 0))
    moved = jax.random.randint(jax.random.fold_in(own, 4), (amount // 2,), 0, 1 << 20) % (margin + 1)
    tallies = tallies.at[source_of].add(-moved).at[taker].add(moved)
    items = jnp.searchsorted(jnp.cumsum(tallies), jnp.arange(rows * top), side="right").astype(jnp.int32)
    table = items.reshape(top, rows).T
    table = table[jax.random.permutation(jax.random.fold_in(own, 1), rows)]
    offset_by = jax.random.randint(jax.random.fold_in(own, 2), (rows, 1), 0, top)
    return jnp.take_along_axis(table, (jnp.arange(top)[None, :] + offset_by) % top, axis=1)


def load_shares(number_of, total, most, lean, full):
    portions = [(1 << 20) // math.isqrt(standing ** lean) + 1 for standing in range(1, number_of + 1)]
    largest = most if full else min(most, max(-(-total // number_of), total * portions[0] // sum(portions)))
    least = 1 if total - largest >= number_of - 1 else 0
    given, spare = [largest] + [least] * (number_of - 1), total - largest - least * (number_of - 1)
    while spare > 0:
        free = [i for i in range(1, number_of) if given[i] < largest] or [i for i in range(1, number_of) if given[i] < most]
        whole, left = sum([portions[i] for i in free]), spare
        for i in free:
            extra = min(most - given[i], max(1, left * portions[i] // whole), spare)
            given[i] = given[i] + extra
            spare = spare - extra
    return np.array(given)


def bell_draw(rng, shape, deviation, limit, split=(), kind=jnp.bfloat16):
    values = jax.random.normal(rng, shape, jnp.float32) * deviation
    if len(split) > 0:
        values = block_levels(rng, shape, split, -0.22, 0.18) * values
    return jnp.clip(values, min=-limit, max=limit).astype(kind)


def setup_inputs(seed: int = 0) -> dict:
    seeds = jax.random.split(jax.random.key(seed), 11)
    tokens = bell_draw(seeds[0], (TOKENS, D), 1.0, 6.0, ((0, 32),))
    route_expert_keys = jax.random.split(jax.random.fold_in(seeds[1], 1), TOKENS // TOK_DEV)
    route_expert_turns = jax.random.permutation(jax.random.fold_in(seeds[1], 3), TOKENS // TOK_DEV)
    route_expert = jax.vmap(lambda own, number: deal_out(jax.random.fold_in(seeds[1], 2), own, number, TOK_DEV, EXPERTS, TOP, CAP, 2))(route_expert_keys, route_expert_turns).reshape((TOKENS, TOP))
    route_weight = jnp.clip(jnp.exp(math.log(1.0) - 2.3025851 * jax.random.uniform(seeds[2], (TOKENS, TOP), jnp.float32) ** block_levels(seeds[2], (TOKENS, TOP), ((0, 32),), -0.2, 0.2)), 0.1, 1.0)
    gate_weight = bell_draw(seeds[3], (EXPERTS, FF, D), D ** -0.5, 0.125, ((0, 32), (1, 8)))
    up_weight = bell_draw(seeds[4], (EXPERTS, FF, D), D ** -0.5, 0.125, ((0, 32), (1, 8)))
    down_weight = bell_draw(seeds[5], (EXPERTS, FF, D), FF ** -0.5, 0.15625, ((0, 32), (1, 8)))
    gate_scale = jnp.clip(jnp.exp(math.log(2.0) - 1.3862944 * jax.random.uniform(seeds[6], (EXPERTS, FF), jnp.float32) ** block_levels(seeds[6], (EXPERTS, FF), ((0, 32), (1, 8)), -0.2, 0.2)), 0.5, 2.0)
    up_scale = jnp.clip(jnp.exp(math.log(2.0) - 1.3862944 * jax.random.uniform(seeds[7], (EXPERTS, FF), jnp.float32) ** block_levels(seeds[7], (EXPERTS, FF), ((0, 32), (1, 8)), -0.2, 0.2)), 0.5, 2.0)
    down_scale = jnp.clip(jnp.exp(jax.random.uniform(seeds[8], (EXPERTS, D), jnp.float32, math.log(0.5), math.log(2.0))), 0.5, 2.0)
    cotangent = bell_draw(seeds[9], (TOKENS, D), 1.0, 6.0, ((0, 32), (1, 8)))
    return {"tokens": tokens, "route_expert": route_expert, "route_weight": route_weight, "gate_weight": gate_weight, "up_weight": up_weight, "down_weight": down_weight, "gate_scale": gate_scale, "up_scale": up_scale, "down_scale": down_scale, "cotangent": cotangent}


def reference(tokens, route_expert, route_weight, gate_weight, up_weight, down_weight, gate_scale, up_scale, down_scale, cotangent):
    assigned = TOKENS * TOP
    bound = N_DP * CAP
    flat_expert = route_expert.reshape(-1).astype(jnp.int32)
    flat_token = (jnp.arange(assigned, dtype=jnp.int32) // TOP).astype(jnp.int32)
    flat_weight = route_weight.reshape(-1)

    def one_expert(carry, expert_id):
        mixed_acc, input_acc, route_acc = carry
        places = jnp.nonzero(flat_expert == expert_id, size=bound, fill_value=assigned)[0].astype(jnp.int32)
        valid = places < assigned
        safe = jnp.minimum(places, assigned - 1).astype(jnp.int32)
        rows_tok = flat_token[safe]
        rows_in = jnp.where(valid[:, None], tokens[rows_tok], jnp.zeros((), tokens.dtype))
        weight_rows = jnp.where(valid, flat_weight[safe], jnp.zeros((), jnp.float32))
        gate_pre = jnp.dot(rows_in, gate_weight[expert_id].T, preferred_element_type=jnp.float32) * gate_scale[expert_id][None, :]
        up_pre = jnp.dot(rows_in, up_weight[expert_id].T, preferred_element_type=jnp.float32) * up_scale[expert_id][None, :]
        sigmoid_gate = jax.nn.sigmoid(gate_pre)
        silu_gate = gate_pre * sigmoid_gate
        hidden = (silu_gate * up_pre).astype(jnp.bfloat16)
        full_out = jnp.dot(hidden, down_weight[expert_id], preferred_element_type=jnp.float32) * down_scale[expert_id][None, :]
        expert_out = full_out.astype(jnp.bfloat16).astype(jnp.float32)
        mixed_acc = mixed_acc.at[rows_tok].add(weight_rows[:, None] * expert_out)
        cot_rows = cotangent[rows_tok].astype(jnp.float32)
        route_rows = jnp.sum(cot_rows * expert_out, axis=1)
        route_acc = route_acc.at[safe].add(jnp.where(valid, route_rows, jnp.zeros((), jnp.float32)))
        out_grad = (cot_rows * weight_rows[:, None] * down_scale[expert_id][None, :]).astype(jnp.bfloat16)
        hidden_grad = jnp.dot(out_grad, down_weight[expert_id].T, preferred_element_type=jnp.float32)
        gate_in = (hidden_grad * up_pre * sigmoid_gate * (1.0 + gate_pre * (1.0 - sigmoid_gate)) * gate_scale[expert_id][None, :]).astype(jnp.bfloat16)
        up_in = (hidden_grad * silu_gate * up_scale[expert_id][None, :]).astype(jnp.bfloat16)
        down_g = jnp.dot(hidden.T, out_grad, preferred_element_type=jnp.float32)
        gate_g = jnp.dot(gate_in.T, rows_in, preferred_element_type=jnp.float32)
        up_g = jnp.dot(up_in.T, rows_in, preferred_element_type=jnp.float32)
        input_part = jnp.dot(gate_in, gate_weight[expert_id], preferred_element_type=jnp.float32)
        input_part = input_part + jnp.dot(up_in, up_weight[expert_id], preferred_element_type=jnp.float32)
        input_acc = input_acc.at[rows_tok].add(jnp.where(valid[:, None], input_part, jnp.zeros((), jnp.float32)))
        return (mixed_acc, input_acc, route_acc), (gate_g, up_g, down_g)

    start = (jnp.zeros((TOKENS, D), jnp.float32), jnp.zeros((TOKENS, D), jnp.float32), jnp.zeros((assigned,), jnp.float32))
    final, grads = lax.scan(one_expert, start, jnp.arange(EXPERTS, dtype=jnp.int32))
    mixed_acc, input_acc, route_acc = final
    gate_grad, up_grad, down_grad = grads
    return (mixed_acc.astype(jnp.bfloat16), input_acc.astype(jnp.bfloat16), route_acc.reshape(TOKENS, TOP), gate_grad, up_grad, down_grad)
```

```python
import functools

import jax
import jax.numpy as jnp
from jax import lax
from jax.experimental import pallas as pl
from jax.experimental.pallas import tpu as pltpu
from jax.sharding import PartitionSpec as P


F32 = jnp.float32
BF16 = jnp.bfloat16
NT = (((1,), (1,)), ((), ()))
NN = (((1,), (0,)), ((), ()))
TN = (((0,), (0,)), ((), ()))


def dot(a, b, dims=NN, **kw):
    return lax.dot_general(a, b, dims, preferred_element_type=F32, **kw)


def cost(flops, nbytes):
    return pl.CostEstimate(flops=flops, bytes_accessed=nbytes, transcendentals=0)


def iota(shape, dim):
    return lax.broadcasted_iota(jnp.int32, shape, dim)


def route_kernel(cap, col_ref, re_ref, rw_ref, cot_ref, ds_ref, m_ref, send_ref):
    choose, toks = re_ref.shape
    experts = ds_ref.shape[0]
    expert_id = iota((experts, toks), 0)
    named = jnp.zeros((experts, toks), F32)
    weight = jnp.zeros((experts, toks), F32)
    for k in range(choose):
        hit = re_ref[k : k + 1, :] == expert_id
        named = named + jnp.where(hit, 1.0, 0.0)
        weight = weight + jnp.where(hit, rw_ref[k : k + 1, :], 0.0)
    before = jnp.where(iota((toks, toks), 0) < iota((toks, toks), 1), 1.0, 0.0).astype(BF16)
    rank = dot(named.astype(BF16), before).astype(jnp.int32)
    code = jnp.where(named > 0.0, rank, -1)
    place = iota((cap, toks), 0)
    slot_weight = []
    for e in range(experts):
        hit = code[e : e + 1, :] == place
        m_ref[e * cap : (e + 1) * cap, :] = jnp.where(hit, 1.0, 0.0).astype(BF16)
        slot_weight.append(
            jnp.sum(jnp.where(hit, weight[e : e + 1, :], 0.0), axis=1, keepdims=True)
        )
    group = 8
    for g in range(experts // group):
        rows = dot(m_ref[g * group * cap : (g + 1) * group * cap, :], cot_ref[...])
        for i in range(group):
            e = g * group + i
            send_ref[e * cap : (e + 1) * cap, :] = (
                rows[i * cap : (i + 1) * cap, :] * slot_weight[e] * ds_ref[e : e + 1, :]
            ).astype(BF16)


def home_kernel(cap, re_ref, rw_ref, mt_ref, mh_ref, ml_ref):
    toks, choose = re_ref.shape
    slots = mt_ref.shape[1]
    experts = slots // cap
    expert_id = iota((toks, experts), 1)
    named = jnp.zeros((toks, experts), F32)
    weight = jnp.zeros((toks, experts), F32)
    for k in range(choose):
        hit = re_ref[:, k : k + 1] == expert_id
        named = named + jnp.where(hit, 1.0, 0.0)
        weight = weight + jnp.where(hit, rw_ref[:, k : k + 1], 0.0)
    before = jnp.where(iota((toks, toks), 1) < iota((toks, toks), 0), 1.0, 0.0).astype(BF16)
    rank = dot(before, named.astype(BF16))
    code = jnp.where(named > 0.0, rank, 128.0).astype(BF16)
    low = iota((experts, slots), 0) * cap
    slot = iota((experts, slots), 1)
    spread = jnp.where((slot >= low) & (slot < low + cap), 1.0, 0.0).astype(BF16)
    high = weight.astype(BF16)
    rest = (weight - high.astype(F32)).astype(BF16)
    place = (iota((toks, slots), 1) & (cap - 1)).astype(F32)
    hit = dot(code, spread) == place
    mt_ref[...] = jnp.where(hit, 1.0, 0.0).astype(BF16)
    mh_ref[...] = jnp.where(hit, dot(high, spread), 0.0).astype(BF16)
    ml_ref[...] = jnp.where(hit, dot(rest, spread), 0.0).astype(BF16)


def forward_kernel(
    e_ref, x_ref, gw_ref, uw_ref, dw_ref, gs_ref, us_ref, ds_ref, g_ref, u_ref, h_ref, y_ref
):
    x = x_ref[...]
    g = dot(x, gw_ref[...], NT) * gs_ref[...]
    u = dot(x, uw_ref[...], NT) * us_ref[...]
    g_ref[...] = g
    u_ref[...] = u
    h = (g * jax.nn.sigmoid(g) * u).astype(BF16)
    h_ref[...] = h
    scale = ds_ref[pl.ds(e_ref[0], 1), :]
    y_ref[...] = (dot(h, dw_ref[...]) * scale).astype(BF16)


def backward_kernel(
    o_ref, g_ref, u_ref, gw_ref, uw_ref, dw_ref, gs_ref, us_ref, gi_ref, ui_ref, p_ref
):
    parts, _, share = o_ref.shape
    hg = dot(o_ref[0], dw_ref[:, :share], NT)
    for c in range(1, parts):
        hg = hg + dot(o_ref[c], dw_ref[:, c * share : (c + 1) * share], NT)
    g = g_ref[...]
    u = u_ref[...]
    s = jax.nn.sigmoid(g)
    gi = (hg * u * s * (1.0 + g * (1.0 - s)) * gs_ref[...]).astype(BF16)
    ui = (hg * (g * s) * us_ref[...]).astype(BF16)
    gi_ref[...] = gi
    ui_ref[...] = ui
    for c in range(parts):
        cols = slice(c * share, (c + 1) * share)
        p_ref[c] = (dot(gi, gw_ref[:, cols]) + dot(ui, uw_ref[:, cols])).astype(BF16)


def combine_kernel(cap, z_ref, y_ref, c_ref, mt_ref, mh_ref, ml_ref, re_ref, o_ref, acc_ref):
    step = pl.program_id(0)
    toks, slots = mt_ref.shape
    experts = slots // cap
    y = y_ref[...]
    o_ref[step, :toks, :] = (dot(mh_ref[...], y) + dot(ml_ref[...], y)).astype(BF16)
    product = dot(c_ref[0], y, NT)

    @pl.when(step == 0)
    def _():
        acc_ref[...] = product

    @pl.when(step > 0)
    def _():
        acc_ref[...] += product

    @pl.when(step == pl.num_programs(0) - 1)
    def _():
        held = jnp.where(mt_ref[...].astype(F32) > 0.0, acc_ref[...], 0.0)
        low = iota((experts, slots), 0) * cap
        slot = iota((experts, slots), 1)
        spread = jnp.where((slot >= low) & (slot < low + cap), 1.0, 0.0)
        table = dot(spread, held, NT, precision=lax.Precision.HIGHEST)
        expert_id = iota((experts, toks), 0)
        lines = [
            jnp.sum(jnp.where(re_ref[k : k + 1, :] == expert_id, table, 0.0), axis=0, keepdims=True)
            for k in range(re_ref.shape[0])
        ]
        block = jnp.concatenate(lines + [jnp.zeros_like(lines[0])] * 4, axis=0)
        block = jnp.concatenate([block, jnp.zeros_like(block)], axis=1).astype(BF16)
        for c in range(o_ref.shape[0]):
            o_ref[c, toks:, :] = block


def mixed_kernel(x_ref, o_ref, r_ref):
    choose, toks = r_ref.shape
    total = x_ref[0].astype(F32)
    for c in range(1, x_ref.shape[0]):
        total = total + x_ref[c].astype(F32)
    o_ref[...] = total[:toks, :].astype(BF16)
    r_ref[...] = total[toks : toks + choose, :toks]


def weight_kernel(x_ref, o_ref, gi_ref, ui_ref, h_ref, gg_ref, ug_ref, dg_ref):
    x = x_ref[...]
    gg_ref[...] = dot(gi_ref[...], x, TN)
    ug_ref[...] = dot(ui_ref[...], x, TN)
    dg_ref[...] = dot(h_ref[...], o_ref[0], TN)


def step(
    tokens,
    route_expert,
    route_weight,
    gate_weight,
    up_weight,
    down_weight,
    gate_scale,
    up_scale,
    down_scale,
    cotangent,
):
    owners = lax.axis_size("dp")
    parts = lax.axis_size("expert")
    toks, width = tokens.shape
    choose = route_expert.shape[1]
    cap = 2 * toks * choose // owners
    slots = owners * cap
    share = width // parts
    hid = gate_weight.shape[1]
    gw, uw, dw = gate_weight[0], up_weight[0], down_weight[0]
    mine = lax.axis_index("dp").astype(jnp.int32).reshape(1)
    col = lax.axis_index("expert").astype(jnp.int32).reshape(1)
    full = lambda *shape: pl.BlockSpec(shape, lambda *_: (0,) * len(shape))
    sds = jax.ShapeDtypeStruct

    onehot, cot_send = pl.pallas_call(
        functools.partial(route_kernel, cap),
        name="route",
        grid_spec=pltpu.PrefetchScalarGridSpec(
            num_scalar_prefetch=1,
            grid=(1,),
            in_specs=[
                full(choose, toks),
                full(choose, toks),
                full(toks, share),
                pl.BlockSpec((owners, share), lambda i, c: (0, c[0])),
            ],
            out_specs=[full(slots, toks), full(slots, share)],
        ),
        out_shape=[sds((slots, toks), BF16), sds((slots, share), BF16)],
        cost_estimate=cost(2 * slots * toks * share, 2 * slots * share * 2),
    )(col, route_expert.T, route_weight.T, cotangent, down_scale)
    cot_mine = lax.all_to_all(
        cot_send.reshape(owners, cap, share), "dp", split_axis=0, concat_axis=0, tiled=True
    ).reshape(slots, share)
    tok_send = lax.dot_general(onehot, tokens, NN, preferred_element_type=BF16)
    arrived = lax.all_to_all(
        tok_send.reshape(owners, cap, width), "dp", split_axis=0, concat_axis=0, tiled=True
    ).reshape(slots, width)
    out_grad = lax.all_gather(cot_mine, "expert", axis=0, tiled=False)

    combine, high, rest = pl.pallas_call(
        functools.partial(home_kernel, cap),
        name="home",
        in_specs=[full(toks, choose)] * 2,
        out_specs=[full(toks, slots)] * 3,
        grid=(1,),
        out_shape=[sds((toks, slots), BF16)] * 3,
        cost_estimate=cost(6 * slots * toks * owners, 6 * slots * toks),
    )(route_expert, route_weight)

    block = 256
    row_hid = pl.BlockSpec((block, hid), lambda i, *_: (i, 0))
    row_wide = pl.BlockSpec((block, width), lambda i, *_: (i, 0))
    g, u, h, out_rows = pl.pallas_call(
        forward_kernel,
        name="forward",
        grid_spec=pltpu.PrefetchScalarGridSpec(
            num_scalar_prefetch=1,
            grid=(slots // block,),
            in_specs=[row_wide]
            + [full(hid, width)] * 3
            + [full(1, hid)] * 2
            + [full(owners, width)],
            out_specs=[row_hid, row_hid, row_hid, row_wide],
        ),
        out_shape=[
            sds((slots, hid), F32),
            sds((slots, hid), F32),
            sds((slots, hid), BF16),
            sds((slots, width), BF16),
        ],
        cost_estimate=cost(6 * slots * width * hid, 4 * slots * width),
    )(mine, arrived, gw, uw, dw, gate_scale, up_scale, down_scale)
    returned = lax.all_to_all(
        out_rows.reshape(owners, cap, width), "dp", split_axis=0, concat_axis=0, tiled=True
    ).reshape(slots, width)

    block = 128
    row_hid = pl.BlockSpec((block, hid), lambda i: (i, 0))
    row_parts = pl.BlockSpec((parts, block, share), lambda i: (0, i, 0))
    gate_in, up_in, input_part = pl.pallas_call(
        backward_kernel,
        name="backward",
        grid=(slots // block,),
        in_specs=[row_parts] + [row_hid] * 2 + [full(hid, width)] * 3 + [full(1, hid)] * 2,
        out_specs=[row_hid, row_hid, row_parts],
        out_shape=[
            sds((slots, hid), BF16),
            sds((slots, hid), BF16),
            sds((parts, slots, share), BF16),
        ],
        cost_estimate=cost(6 * slots * width * hid, 4 * slots * width),
    )(out_grad, g, u, gw, uw, dw, gate_scale, up_scale)
    input_cols = lax.psum_scatter(
        input_part.reshape(parts * slots, share), "expert", scatter_dimension=0, tiled=True
    )

    col_wide = pl.BlockSpec((slots, share), lambda i: (0, i))
    col_hid = pl.BlockSpec((hid, share), lambda i: (0, i))
    gate_grad, up_grad, down_grad = pl.pallas_call(
        weight_kernel,
        name="weight",
        grid=(parts,),
        in_specs=[col_wide, pl.BlockSpec((1, slots, share), lambda i: (i, 0, 0))]
        + [full(slots, hid)] * 3,
        out_specs=[col_hid] * 3,
        out_shape=[sds((hid, width), F32)] * 3,
        cost_estimate=cost(6 * slots * width * hid, 4 * slots * width + 12 * hid * width),
    )(arrived, out_grad, gate_in, up_in, h)

    raw = [cotangent] + [
        lax.ppermute(cotangent, "expert", [(i, (i + s) % parts) for i in range(parts)])
        for s in range(1, parts)
    ]
    raw = jnp.stack(raw)
    tail = 8
    mixed_part = pl.pallas_call(
        functools.partial(combine_kernel, cap),
        name="combine",
        grid_spec=pltpu.PrefetchScalarGridSpec(
            num_scalar_prefetch=1,
            grid=(parts,),
            in_specs=[
                pl.BlockSpec((slots, share), lambda i, z: (0, i)),
                pl.BlockSpec((1, toks, share), lambda i, z: ((z[0] + parts - i) % parts, 0, 0)),
            ]
            + [full(toks, slots)] * 3
            + [full(choose, toks)],
            out_specs=full(parts, toks + tail, share),
            scratch_shapes=[pltpu.VMEM((toks, slots), F32)],
        ),
        out_shape=sds((parts, toks + tail, share), BF16),
        cost_estimate=cost(6 * slots * toks * width, 2 * slots * width),
    )(col, returned, raw, combine, high, rest, route_expert.T)
    mixed_all = lax.all_to_all(mixed_part, "expert", split_axis=0, concat_axis=0, tiled=True)
    mixed, route_grad = pl.pallas_call(
        mixed_kernel,
        name="mixed",
        grid=(1,),
        in_specs=[full(parts, toks + tail, share)],
        out_specs=[full(toks, share), full(choose, toks)],
        out_shape=[sds((toks, share), BF16), sds((choose, toks), F32)],
        cost_estimate=cost(parts * toks * share, 2 * parts * toks * share),
    )(mixed_all)
    route_grad = route_grad.T
    input_home = lax.all_to_all(
        input_cols.reshape(owners, cap, share), "dp", split_axis=0, concat_axis=0, tiled=True
    ).reshape(slots, share)
    token_grad = dot(combine, input_home).astype(BF16)
    return (mixed, token_grad, route_grad, gate_grad[None], up_grad[None], down_grad[None])


def solution(mesh):
    return jax.shard_map(
        step,
        mesh=mesh,
        in_specs=(
            P("dp", None),
            P("dp", None),
            P("dp", None),
            P("dp", "expert", None),
            P("dp", "expert", None),
            P("dp", "expert", None),
            P("dp", "expert"),
            P("dp", "expert"),
            P(),
            P("dp", "expert"),
        ),
        out_specs=(
            P("dp", "expert"),
            P("dp", "expert"),
            P("dp", None),
            P("dp", "expert", None),
            P("dp", "expert", None),
            P("dp", "expert", None),
        ),
        check_vma=False,
    )
```

```python
import functools

import jax
import jax.numpy as jnp
from jax import lax
from jax.experimental import pallas as pl
from jax.experimental.pallas import tpu as pltpu
from jax.sharding import PartitionSpec as P


F32 = jnp.float32
BF16 = jnp.bfloat16
NT = (((1,), (1,)), ((), ()))
NN = (((1,), (0,)), ((), ()))
TN = (((0,), (0,)), ((), ()))


def dot(a, b, dims=NN, **kw):
    return lax.dot_general(a, b, dims, preferred_element_type=F32, **kw)


def cost(flops, nbytes):
    return pl.CostEstimate(flops=flops, bytes_accessed=nbytes, transcendentals=0)


def iota(shape, dim):
    return lax.broadcasted_iota(jnp.int32, shape, dim)


def route_kernel(cap, col_ref, re_ref, rw_ref, cot_ref, ds_ref, m_ref, send_ref):
    choose, toks = re_ref.shape
    experts = ds_ref.shape[0]
    expert_id = iota((experts, toks), 0)
    named = jnp.zeros((experts, toks), F32)
    weight = jnp.zeros((experts, toks), F32)
    for k in range(choose):
        hit = re_ref[k : k + 1, :] == expert_id
        named = named + jnp.where(hit, 1.0, 0.0)
        weight = weight + jnp.where(hit, rw_ref[k : k + 1, :], 0.0)
    before = jnp.where(iota((toks, toks), 0) < iota((toks, toks), 1), 1.0, 0.0).astype(BF16)
    rank = dot(named.astype(BF16), before).astype(jnp.int32)
    code = jnp.where(named > 0.0, rank, -1)
    place = iota((cap, toks), 0)
    slot_weight = []
    for e in range(experts):
        hit = code[e : e + 1, :] == place
        m_ref[e * cap : (e + 1) * cap, :] = jnp.where(hit, 1.0, 0.0).astype(BF16)
        slot_weight.append(
            jnp.sum(jnp.where(hit, weight[e : e + 1, :], 0.0), axis=1, keepdims=True)
        )
    group = 8
    for g in range(experts // group):
        rows = dot(m_ref[g * group * cap : (g + 1) * group * cap, :], cot_ref[...])
        for i in range(group):
            e = g * group + i
            send_ref[e * cap : (e + 1) * cap, :] = (
                rows[i * cap : (i + 1) * cap, :] * slot_weight[e] * ds_ref[e : e + 1, :]
            ).astype(BF16)


def home_kernel(cap, re_ref, rw_ref, mt_ref, mh_ref, ml_ref):
    toks, choose = re_ref.shape
    slots = mt_ref.shape[1]
    experts = slots // cap
    expert_id = iota((toks, experts), 1)
    named = jnp.zeros((toks, experts), F32)
    weight = jnp.zeros((toks, experts), F32)
    for k in range(choose):
        hit = re_ref[:, k : k + 1] == expert_id
        named = named + jnp.where(hit, 1.0, 0.0)
        weight = weight + jnp.where(hit, rw_ref[:, k : k + 1], 0.0)
    before = jnp.where(iota((toks, toks), 1) < iota((toks, toks), 0), 1.0, 0.0).astype(BF16)
    rank = dot(before, named.astype(BF16))
    code = jnp.where(named > 0.0, rank, 128.0).astype(BF16)
    low = iota((experts, slots), 0) * cap
    slot = iota((experts, slots), 1)
    spread = jnp.where((slot >= low) & (slot < low + cap), 1.0, 0.0).astype(BF16)
    high = weight.astype(BF16)
    rest = (weight - high.astype(F32)).astype(BF16)
    place = (iota((toks, slots), 1) & (cap - 1)).astype(F32)
    hit = dot(code, spread) == place
    mt_ref[...] = jnp.where(hit, 1.0, 0.0).astype(BF16)
    mh_ref[...] = jnp.where(hit, dot(high, spread), 0.0).astype(BF16)
    ml_ref[...] = jnp.where(hit, dot(rest, spread), 0.0).astype(BF16)


def forward_kernel(
    e_ref, x_ref, gw_ref, uw_ref, dw_ref, gs_ref, us_ref, ds_ref, g_ref, u_ref, h_ref, y_ref
):
    x = x_ref[...]
    g = dot(x, gw_ref[...], NT) * gs_ref[...]
    u = dot(x, uw_ref[...], NT) * us_ref[...]
    g_ref[...] = g
    u_ref[...] = u
    h = (g * jax.nn.sigmoid(g) * u).astype(BF16)
    h_ref[...] = h
    scale = ds_ref[pl.ds(e_ref[0], 1), :]
    y_ref[...] = (dot(h, dw_ref[...]) * scale).astype(BF16)


def backward_kernel(parts, z_ref, *refs):
    o_refs = refs[:parts]
    g_ref, u_ref, gw_ref, uw_ref, dw_ref, gs_ref, us_ref, gi_ref, ui_ref, p_ref = refs[parts:]
    share = p_ref.shape[2]

    def cols(c):
        at = lax.rem(z_ref[0] + c, parts)
        return pl.ds(pl.multiple_of(at * share, share), share)

    hg = dot(o_refs[0][...], dw_ref[:, cols(0)], NT)
    for c in range(1, parts):
        hg = hg + dot(o_refs[c][...], dw_ref[:, cols(parts - c)], NT)
    g = g_ref[...]
    u = u_ref[...]
    s = jax.nn.sigmoid(g)
    gi = (hg * u * s * (1.0 + g * (1.0 - s)) * gs_ref[...]).astype(BF16)
    ui = (hg * (g * s) * us_ref[...]).astype(BF16)
    gi_ref[...] = gi
    ui_ref[...] = ui
    for c in range(parts):
        p_ref[c] = (dot(gi, gw_ref[:, cols(c)]) + dot(ui, uw_ref[:, cols(c)])).astype(BF16)


def combine_kernel(cap, z_ref, y_ref, c_ref, mt_ref, mh_ref, ml_ref, re_ref, o_ref, acc_ref):
    step = pl.program_id(0)
    toks, slots = mt_ref.shape
    experts = slots // cap
    y = y_ref[...]
    parts = o_ref.shape[0]
    at = lax.rem(z_ref[0] + parts - step, parts)
    o_ref[at, :toks, :] = (dot(mh_ref[...], y) + dot(ml_ref[...], y)).astype(BF16)
    product = dot(c_ref[...].reshape(toks, y.shape[1]), y, NT)

    @pl.when(step == 0)
    def _():
        acc_ref[...] = product

    @pl.when(step > 0)
    def _():
        acc_ref[...] += product

    @pl.when(step == pl.num_programs(0) - 1)
    def _():
        held = jnp.where(mt_ref[...].astype(F32) > 0.0, acc_ref[...], 0.0)
        low = iota((experts, slots), 0) * cap
        slot = iota((experts, slots), 1)
        spread = jnp.where((slot >= low) & (slot < low + cap), 1.0, 0.0)
        table = dot(spread, held, NT, precision=lax.Precision.HIGHEST)
        expert_id = iota((experts, toks), 0)
        lines = [
            jnp.sum(jnp.where(re_ref[k : k + 1, :] == expert_id, table, 0.0), axis=0, keepdims=True)
            for k in range(re_ref.shape[0])
        ]
        block = jnp.concatenate(lines + [jnp.zeros_like(lines[0])] * 4, axis=0)
        block = jnp.concatenate([block, jnp.zeros_like(block)], axis=1).astype(BF16)
        for c in range(o_ref.shape[0]):
            o_ref[c, toks:, :] = block


def mixed_kernel(x_ref, o_ref, r_ref):
    choose, toks = r_ref.shape
    total = x_ref[0].astype(F32)
    for c in range(1, x_ref.shape[0]):
        total = total + x_ref[c].astype(F32)
    o_ref[...] = total[:toks, :].astype(BF16)
    r_ref[...] = total[toks : toks + choose, :toks]


def weight_kernel(x_ref, *refs):
    gi_refs, ui_refs, gg_ref, ug_ref = refs[:2], refs[2:4], refs[4], refs[5]
    x = x_ref[...]
    gg_ref[...] = dot(jnp.concatenate([r[...] for r in gi_refs], axis=0), x, TN)
    ug_ref[...] = dot(jnp.concatenate([r[...] for r in ui_refs], axis=0), x, TN)


def down_kernel(parts, z_ref, h_ref, *refs):
    dg_ref = refs[-1]
    share = refs[0].shape[1]
    rows = h_ref.shape[0] // 2
    h = h_ref[...]
    for c in range(parts):
        o = jnp.concatenate([refs[c][:rows, :], refs[parts + c][:rows, :]], axis=0)
        at = lax.rem(z_ref[0] + (parts - c), parts)
        dg_ref[:, pl.ds(pl.multiple_of(at * share, share), share)] = dot(h, o, TN)


def shift(x, by):
    size = lax.axis_size("expert")
    return lax.ppermute(x, "expert", [(i, (i + by) % size) for i in range(size)])


def ring_gather(first, second):
    size = lax.axis_size("expert")
    half = size // 2
    pieces = [[None] * size, [None] * size]
    for j, (x, ups) in enumerate(((first, half), (second, half - 1))):
        pieces[j][0] = x
        up = down = x
        for k in range(1, half + 1):
            if k <= ups:
                up = shift(up, 1)
                pieces[j][k] = up
            if k <= size - 1 - ups:
                down = shift(down, -1)
                pieces[j][size - k] = down
    return pieces


def add(*terms):
    return sum(t.astype(F32) for t in terms).astype(BF16)


def ring_scatter(halves):
    sums = []
    for parts, ups in zip(halves, (4, 3)):
        size = parts.shape[0]
        up = shift(parts[ups], 1)
        down = shift(parts[ups + 1], -1)
        for k in range(ups - 1, 0, -1):
            up = shift(add(up, parts[k]), 1)
        for k in range(ups + 2, size):
            down = shift(add(down, parts[k]), -1)
        sums.append(add(up, down, parts[0]))
    return jnp.concatenate(sums, axis=0)


def step(
    tokens,
    route_expert,
    route_weight,
    gate_weight,
    up_weight,
    down_weight,
    gate_scale,
    up_scale,
    down_scale,
    cotangent,
):
    owners = lax.axis_size("dp")
    parts = lax.axis_size("expert")
    toks, width = tokens.shape
    choose = route_expert.shape[1]
    cap = 2 * toks * choose // owners
    slots = owners * cap
    share = width // parts
    hid = gate_weight.shape[1]
    gw, uw, dw = gate_weight[0], up_weight[0], down_weight[0]
    mine = lax.axis_index("dp").astype(jnp.int32).reshape(1)
    col = lax.axis_index("expert").astype(jnp.int32).reshape(1)
    full = lambda *shape: pl.BlockSpec(shape, lambda *_: (0,) * len(shape))
    sds = jax.ShapeDtypeStruct

    onehot, cot_send = pl.pallas_call(
        functools.partial(route_kernel, cap),
        name="route",
        grid_spec=pltpu.PrefetchScalarGridSpec(
            num_scalar_prefetch=1,
            grid=(1,),
            in_specs=[
                full(choose, toks),
                full(choose, toks),
                full(toks, share),
                pl.BlockSpec((owners, share), lambda i, c: (0, c[0])),
            ],
            out_specs=[full(slots, toks), full(slots, share)],
        ),
        out_shape=[sds((slots, toks), BF16), sds((slots, share), BF16)],
        cost_estimate=cost(2 * slots * toks * share, 2 * slots * share * 2),
    )(col, route_expert.T, route_weight.T, cotangent, down_scale)
    cot_mine = lax.all_to_all(
        cot_send.reshape(owners, cap, share), "dp", split_axis=0, concat_axis=0, tiled=True
    ).reshape(slots, share)
    tok_send = lax.dot_general(onehot, tokens, NN, preferred_element_type=BF16)
    arrived = lax.all_to_all(
        tok_send.reshape(owners, cap, width), "dp", split_axis=0, concat_axis=0, tiled=True
    ).reshape(slots, width)
    rows, raw = slots // 2, toks // 2
    out_grad = ring_gather(
        jnp.concatenate([cot_mine[:rows], cotangent[:raw]], axis=0),
        jnp.concatenate([cot_mine[rows:], cotangent[raw:]], axis=0),
    )

    combine, high, rest = pl.pallas_call(
        functools.partial(home_kernel, cap),
        name="home",
        in_specs=[full(toks, choose)] * 2,
        out_specs=[full(toks, slots)] * 3,
        grid=(1,),
        out_shape=[sds((toks, slots), BF16)] * 3,
        cost_estimate=cost(6 * slots * toks * owners, 6 * slots * toks),
    )(route_expert, route_weight)

    block = 256
    row_hid = pl.BlockSpec((block, hid), lambda i, *_: (i, 0))
    row_wide = pl.BlockSpec((block, width), lambda i, *_: (i, 0))
    g, u, h, out_rows = pl.pallas_call(
        forward_kernel,
        name="forward",
        grid_spec=pltpu.PrefetchScalarGridSpec(
            num_scalar_prefetch=1,
            grid=(slots // block,),
            in_specs=[row_wide]
            + [full(hid, width)] * 3
            + [full(1, hid)] * 2
            + [full(owners, width)],
            out_specs=[row_hid, row_hid, row_hid, row_wide],
        ),
        out_shape=[
            sds((slots, hid), F32),
            sds((slots, hid), F32),
            sds((slots, hid), BF16),
            sds((slots, width), BF16),
        ],
        cost_estimate=cost(6 * slots * width * hid, 4 * slots * width),
    )(mine, arrived, gw, uw, dw, gate_scale, up_scale, down_scale)
    returned = lax.all_to_all(
        out_rows.reshape(owners, cap, width), "dp", split_axis=0, concat_axis=0, tiled=True
    ).reshape(slots, width)

    block = 256
    per = rows // block
    halves = []
    for j in range(2):
        row_in = pl.BlockSpec((block, hid), lambda i, z, j=j: (i + j * per, 0))
        row_out = pl.BlockSpec((block, hid), lambda i, z: (i, 0))
        halves.append(
            pl.pallas_call(
                functools.partial(backward_kernel, parts),
                name="backward",
                grid_spec=pltpu.PrefetchScalarGridSpec(
                    num_scalar_prefetch=1,
                    grid=(per,),
                    in_specs=[pl.BlockSpec((block, share), lambda i, z: (i, 0))] * parts
                    + [row_in] * 2
                    + [full(hid, width)] * 3
                    + [full(1, hid)] * 2,
                    out_specs=[
                        row_out,
                        row_out,
                        pl.BlockSpec((parts, block, share), lambda i, z: (0, i, 0)),
                    ],
                ),
                out_shape=[
                    sds((rows, hid), BF16),
                    sds((rows, hid), BF16),
                    sds((parts, rows, share), BF16),
                ],
                cost_estimate=cost(3 * slots * width * hid, 2 * slots * width),
            )(col, *out_grad[j], g, u, gw, uw, dw, gate_scale, up_scale)
        )
    input_cols = ring_scatter([half[2] for half in halves])

    col_hid = pl.BlockSpec((hid, share), lambda i: (0, i))
    gate_grad, up_grad = pl.pallas_call(
        weight_kernel,
        name="weight",
        grid=(parts,),
        in_specs=[pl.BlockSpec((slots, share), lambda i: (0, i))] + [full(rows, hid)] * 4,
        out_specs=[col_hid] * 2,
        out_shape=[sds((hid, width), F32)] * 2,
        cost_estimate=cost(4 * slots * width * hid, 2 * slots * width + 8 * hid * width),
    )(arrived, halves[0][0], halves[1][0], halves[0][1], halves[1][1])
    down_grad = pl.pallas_call(
        functools.partial(down_kernel, parts),
        name="down",
        grid_spec=pltpu.PrefetchScalarGridSpec(
            num_scalar_prefetch=1,
            grid=(1,),
            in_specs=[full(slots, hid)] + [full(rows + raw, share)] * (2 * parts),
            out_specs=full(hid, width),
        ),
        out_shape=sds((hid, width), F32),
        cost_estimate=cost(2 * slots * width * hid, 2 * slots * width + 4 * hid * width),
    )(col, h, *out_grad[0], *out_grad[1])

    raw_all = jnp.stack([o[rows:] for pair in zip(*out_grad) for o in pair])
    raw_all = raw_all.reshape(parts, 2, raw, share)
    tail = 8
    mixed_part = pl.pallas_call(
        functools.partial(combine_kernel, cap),
        name="combine",
        grid_spec=pltpu.PrefetchScalarGridSpec(
            num_scalar_prefetch=1,
            grid=(parts,),
            in_specs=[
                pl.BlockSpec((slots, share), lambda i, z: (0, lax.rem(z[0] + parts - i, parts))),
                pl.BlockSpec((None, 2, raw, share), lambda i, z: (i, 0, 0, 0)),
            ]
            + [full(toks, slots)] * 3
            + [full(choose, toks)],
            out_specs=full(parts, toks + tail, share),
            scratch_shapes=[pltpu.VMEM((toks, slots), F32)],
        ),
        out_shape=sds((parts, toks + tail, share), BF16),
        cost_estimate=cost(6 * slots * toks * width, 2 * slots * width),
    )(col, returned, raw_all, combine, high, rest, route_expert.T)
    mixed_all = lax.all_to_all(mixed_part, "expert", split_axis=0, concat_axis=0, tiled=True)
    mixed, route_grad = pl.pallas_call(
        mixed_kernel,
        name="mixed",
        grid=(1,),
        in_specs=[full(parts, toks + tail, share)],
        out_specs=[full(toks, share), full(choose, toks)],
        out_shape=[sds((toks, share), BF16), sds((choose, toks), F32)],
        cost_estimate=cost(parts * toks * share, 2 * parts * toks * share),
    )(mixed_all)
    route_grad = route_grad.T
    input_home = lax.all_to_all(
        input_cols.reshape(owners, cap, share), "dp", split_axis=0, concat_axis=0, tiled=True
    ).reshape(slots, share)
    token_grad = dot(combine, input_home).astype(BF16)
    return (mixed, token_grad, route_grad, gate_grad[None], up_grad[None], down_grad[None])


def solution(mesh):
    return jax.shard_map(
        step,
        mesh=mesh,
        in_specs=(
            P("dp", None),
            P("dp", None),
            P("dp", None),
            P("dp", "expert", None),
            P("dp", "expert", None),
            P("dp", "expert", None),
            P("dp", "expert"),
            P("dp", "expert"),
            P(),
            P("dp", "expert"),
        ),
        out_specs=(
            P("dp", "expert"),
            P("dp", "expert"),
            P("dp", None),
            P("dp", "expert", None),
            P("dp", "expert", None),
            P("dp", "expert", None),
        ),
        check_vma=False,
    )
```

```python
import functools

import jax
import jax.numpy as jnp
from jax import lax
from jax.experimental import pallas as pl
from jax.experimental.pallas import tpu as pltpu
from jax.sharding import PartitionSpec as P


F32 = jnp.float32
BF16 = jnp.bfloat16
NT = (((1,), (1,)), ((), ()))
NN = (((1,), (0,)), ((), ()))
TN = (((0,), (0,)), ((), ()))


def dot(a, b, dims=NN, **kw):
    return lax.dot_general(a, b, dims, preferred_element_type=F32, **kw)


def cost(flops, nbytes):
    return pl.CostEstimate(flops=flops, bytes_accessed=nbytes, transcendentals=0)


def iota(shape, dim):
    return lax.broadcasted_iota(jnp.int32, shape, dim)


def route_kernel(cap, col_ref, re_ref, rw_ref, cot_ref, ds_ref, m_ref, send_ref):
    choose, toks = re_ref.shape
    experts = ds_ref.shape[0]
    expert_id = iota((experts, toks), 0)
    named = jnp.zeros((experts, toks), F32)
    weight = jnp.zeros((experts, toks), F32)
    for k in range(choose):
        hit = re_ref[k : k + 1, :] == expert_id
        named = named + jnp.where(hit, 1.0, 0.0)
        weight = weight + jnp.where(hit, rw_ref[k : k + 1, :], 0.0)
    before = jnp.where(iota((toks, toks), 0) < iota((toks, toks), 1), 1.0, 0.0).astype(BF16)
    rank = dot(named.astype(BF16), before).astype(jnp.int32)
    code = jnp.where(named > 0.0, rank, -1)
    place = iota((cap, toks), 0)
    slot_weight = []
    for e in range(experts):
        hit = code[e : e + 1, :] == place
        m_ref[e * cap : (e + 1) * cap, :] = jnp.where(hit, 1.0, 0.0).astype(BF16)
        slot_weight.append(
            jnp.sum(jnp.where(hit, weight[e : e + 1, :], 0.0), axis=1, keepdims=True)
        )
    group = 8
    for g in range(experts // group):
        rows = dot(m_ref[g * group * cap : (g + 1) * group * cap, :], cot_ref[...])
        for i in range(group):
            e = g * group + i
            send_ref[e * cap : (e + 1) * cap, :] = (
                rows[i * cap : (i + 1) * cap, :] * slot_weight[e] * ds_ref[e : e + 1, :]
            ).astype(BF16)


def home_kernel(cap, re_ref, rw_ref, mt_ref, mw_ref):
    toks, choose = re_ref.shape
    slots = mt_ref.shape[1]
    experts = slots // cap
    expert_id = iota((toks, experts), 1)
    named = jnp.zeros((toks, experts), F32)
    weight = jnp.zeros((toks, experts), F32)
    for k in range(choose):
        hit = re_ref[:, k : k + 1] == expert_id
        named = named + jnp.where(hit, 1.0, 0.0)
        weight = weight + jnp.where(hit, rw_ref[:, k : k + 1], 0.0)
    before = jnp.where(iota((toks, toks), 1) < iota((toks, toks), 0), 1.0, 0.0).astype(BF16)
    rank = dot(before, named.astype(BF16))
    code = jnp.where(named > 0.0, rank, 128.0).astype(BF16)
    low = iota((experts, slots), 0) * cap
    slot = iota((experts, slots), 1)
    spread = jnp.where((slot >= low) & (slot < low + cap), 1.0, 0.0).astype(BF16)
    high = weight.astype(BF16)
    rest = (weight - high.astype(F32)).astype(BF16)
    place = (iota((toks, slots), 1) & (cap - 1)).astype(F32)
    hit = dot(code, spread) == place
    mt_ref[...] = jnp.where(hit, 1.0, 0.0).astype(BF16)
    mw_ref[:toks, :] = jnp.where(hit, dot(high, spread), 0.0).astype(BF16)
    mw_ref[toks:, :] = jnp.where(hit, dot(rest, spread), 0.0).astype(BF16)


def forward_kernel(
    e_ref, x_ref, gw_ref, uw_ref, dw_ref, gs_ref, us_ref, ds_ref, g_ref, u_ref, h_ref, y_ref
):
    x = x_ref[...]
    g = dot(x, gw_ref[...], NT) * gs_ref[...]
    u = dot(x, uw_ref[...], NT) * us_ref[...]
    g_ref[...] = g
    u_ref[...] = u
    h = (g * jax.nn.sigmoid(g) * u).astype(BF16)
    h_ref[...] = h
    scale = ds_ref[pl.ds(e_ref[0], 1), :]
    y_ref[...] = (dot(h, dw_ref[...]) * scale).astype(BF16)


def backward_kernel(parts, z_ref, *refs):
    o_refs = refs[:parts]
    g_ref, u_ref, gw_ref, uw_ref, dw_ref, gs_ref, us_ref, gi_ref, ui_ref = refs[parts:-parts]
    p_refs = refs[-parts:]
    share = p_refs[0].shape[1]

    def cols(c):
        at = lax.rem(z_ref[0] + c, parts)
        return pl.ds(pl.multiple_of(at * share, share), share)

    hg = dot(o_refs[0][...], dw_ref[:, cols(0)], NT)
    for c in range(1, parts):
        hg = hg + dot(o_refs[c][...], dw_ref[:, cols(parts - c)], NT)
    g = g_ref[...]
    u = u_ref[...]
    s = jax.nn.sigmoid(g)
    gi = (hg * u * s * (1.0 + g * (1.0 - s)) * gs_ref[...]).astype(BF16)
    ui = (hg * (g * s) * us_ref[...]).astype(BF16)
    gi_ref[...] = gi
    ui_ref[...] = ui
    for c in range(parts):
        p_refs[c][...] = (dot(gi, gw_ref[:, cols(c)]) + dot(ui, uw_ref[:, cols(c)])).astype(BF16)


def combine_kernel(cap, parts, z_ref, y_ref, mt_ref, mw_ref, re_ref, *refs):
    o_ref, acc_ref, prod_ref = refs[2 * parts :]
    step = pl.program_id(0)
    toks, slots = mt_ref.shape
    experts = slots // cap
    block = y_ref.shape[0]
    share = refs[0].shape[1]
    part = dot(mw_ref[...], y_ref[...])

    @pl.when(step == 0)
    def _():
        acc_ref[...] = part

    @pl.when(step > 0)
    def _():
        acc_ref[...] += part

    prod = None
    for k in range(parts):
        at = lax.rem(z_ref[0] + (parts - k), parts)
        cols = pl.ds(pl.multiple_of(at * share, share), share)
        c = jnp.concatenate([refs[k][...], refs[parts + k][...]], axis=0)
        term = dot(c, y_ref[:, cols], NT)
        prod = term if prod is None else prod + term
    prod_ref[:, pl.ds(pl.multiple_of(step * block, block), block)] = prod

    @pl.when(step == pl.num_programs(0) - 1)
    def _():
        held = jnp.where(mt_ref[...].astype(F32) > 0.0, prod_ref[...], 0.0)
        low = iota((experts, slots), 0) * cap
        slot = iota((experts, slots), 1)
        spread = jnp.where((slot >= low) & (slot < low + cap), 1.0, 0.0)
        table = dot(spread, held, NT, precision=lax.Precision.HIGHEST)
        expert_id = iota((experts, toks), 0)
        lines = [
            jnp.sum(jnp.where(re_ref[k : k + 1, :] == expert_id, table, 0.0), axis=0, keepdims=True)
            for k in range(re_ref.shape[0])
        ]
        tail = jnp.concatenate(lines + [jnp.zeros_like(lines[0])] * 4, axis=0)
        tail = jnp.concatenate([tail, jnp.zeros_like(tail)], axis=1).astype(BF16)
        for c in range(parts):
            cols = slice(c * share, (c + 1) * share)
            o_ref[c, :toks, :] = (acc_ref[:toks, cols] + acc_ref[toks:, cols]).astype(BF16)
            o_ref[c, toks:, :] = tail


def mixed_kernel(x_ref, o_ref, r_ref):
    choose, toks = r_ref.shape
    total = x_ref[0].astype(F32)
    for c in range(1, x_ref.shape[0]):
        total = total + x_ref[c].astype(F32)
    o_ref[...] = total[:toks, :].astype(BF16)
    r_ref[...] = total[toks : toks + choose, :toks]


def weight_kernel(x_ref, *refs):
    gi_refs, ui_refs, gg_ref, ug_ref = refs[:2], refs[2:4], refs[4], refs[5]
    x = x_ref[...]
    gg_ref[...] = dot(jnp.concatenate([r[...] for r in gi_refs], axis=0), x, TN)
    ug_ref[...] = dot(jnp.concatenate([r[...] for r in ui_refs], axis=0), x, TN)


def down_kernel(parts, z_ref, h_ref, *refs):
    dg_ref = refs[-1]
    share = refs[0].shape[1]
    rows = h_ref.shape[0] // 2
    h = h_ref[...]
    for c in range(parts):
        o = jnp.concatenate([refs[c][:rows, :], refs[parts + c][:rows, :]], axis=0)
        at = lax.rem(z_ref[0] + (parts - c), parts)
        dg_ref[:, pl.ds(pl.multiple_of(at * share, share), share)] = dot(h, o, TN)


def shift(x, by):
    size = lax.axis_size("expert")
    return lax.ppermute(x, "expert", [(i, (i + by) % size) for i in range(size)])


def ring_gather(first, second):
    size = lax.axis_size("expert")
    half = size // 2
    pieces = [[None] * size, [None] * size]
    for j, (x, ups) in enumerate(((first, half), (second, half - 1))):
        pieces[j][0] = x
        up = down = x
        for k in range(1, half + 1):
            if k <= ups:
                up = shift(up, 1)
                pieces[j][k] = up
            if k <= size - 1 - ups:
                down = shift(down, -1)
                pieces[j][size - k] = down
    return pieces


def add(*terms):
    return sum(t.astype(F32) for t in terms).astype(BF16)


def ring_scatter(halves):
    sums = []
    for parts, ups in zip(halves, (4, 3)):
        size = len(parts)
        up = shift(parts[ups], 1)
        down = shift(parts[ups + 1], -1)
        for k in range(ups - 1, 0, -1):
            up = shift(add(up, parts[k]), 1)
        for k in range(ups + 2, size):
            down = shift(add(down, parts[k]), -1)
        sums.append(add(up, down, parts[0]))
    return jnp.concatenate(sums, axis=0)


def step(
    tokens,
    route_expert,
    route_weight,
    gate_weight,
    up_weight,
    down_weight,
    gate_scale,
    up_scale,
    down_scale,
    cotangent,
):
    owners = lax.axis_size("dp")
    parts = lax.axis_size("expert")
    toks, width = tokens.shape
    choose = route_expert.shape[1]
    cap = 2 * toks * choose // owners
    slots = owners * cap
    share = width // parts
    hid = gate_weight.shape[1]
    gw, uw, dw = gate_weight[0], up_weight[0], down_weight[0]
    mine = lax.axis_index("dp").astype(jnp.int32).reshape(1)
    col = lax.axis_index("expert").astype(jnp.int32).reshape(1)
    full = lambda *shape: pl.BlockSpec(shape, lambda *_: (0,) * len(shape))
    sds = jax.ShapeDtypeStruct

    onehot, cot_send = pl.pallas_call(
        functools.partial(route_kernel, cap),
        name="route",
        grid_spec=pltpu.PrefetchScalarGridSpec(
            num_scalar_prefetch=1,
            grid=(1,),
            in_specs=[
                full(choose, toks),
                full(choose, toks),
                full(toks, share),
                pl.BlockSpec((owners, share), lambda i, c: (0, c[0])),
            ],
            out_specs=[full(slots, toks), full(slots, share)],
        ),
        out_shape=[sds((slots, toks), BF16), sds((slots, share), BF16)],
        cost_estimate=cost(2 * slots * toks * share, 2 * slots * share * 2),
    )(col, route_expert.T, route_weight.T, cotangent, down_scale)
    cot_mine = lax.all_to_all(
        cot_send.reshape(owners, cap, share), "dp", split_axis=0, concat_axis=0, tiled=True
    ).reshape(slots, share)
    tok_send = lax.dot_general(onehot, tokens, NN, preferred_element_type=BF16)
    arrived = lax.all_to_all(
        tok_send.reshape(owners, cap, width), "dp", split_axis=0, concat_axis=0, tiled=True
    ).reshape(slots, width)
    rows, raw = slots // 2, toks // 2
    out_grad = ring_gather(
        jnp.concatenate([cot_mine[:rows], cotangent[:raw]], axis=0),
        jnp.concatenate([cot_mine[rows:], cotangent[raw:]], axis=0),
    )

    combine, weighted = pl.pallas_call(
        functools.partial(home_kernel, cap),
        name="home",
        in_specs=[full(toks, choose)] * 2,
        out_specs=[full(toks, slots), full(2 * toks, slots)],
        grid=(1,),
        out_shape=[sds((toks, slots), BF16), sds((2 * toks, slots), BF16)],
        cost_estimate=cost(6 * slots * toks * owners, 6 * slots * toks),
    )(route_expert, route_weight)

    block = 256
    row_hid = pl.BlockSpec((block, hid), lambda i, *_: (i, 0))
    row_wide = pl.BlockSpec((block, width), lambda i, *_: (i, 0))
    g, u, h, out_rows = pl.pallas_call(
        forward_kernel,
        name="forward",
        grid_spec=pltpu.PrefetchScalarGridSpec(
            num_scalar_prefetch=1,
            grid=(slots // block,),
            in_specs=[row_wide]
            + [full(hid, width)] * 3
            + [full(1, hid)] * 2
            + [full(owners, width)],
            out_specs=[row_hid, row_hid, row_hid, row_wide],
        ),
        out_shape=[
            sds((slots, hid), F32),
            sds((slots, hid), F32),
            sds((slots, hid), BF16),
            sds((slots, width), BF16),
        ],
        cost_estimate=cost(6 * slots * width * hid, 4 * slots * width),
    )(mine, arrived, gw, uw, dw, gate_scale, up_scale, down_scale)
    returned = lax.all_to_all(
        out_rows.reshape(owners, cap, width), "dp", split_axis=0, concat_axis=0, tiled=True
    ).reshape(slots, width)

    block = 256
    per = rows // block
    halves = []
    for j in range(2):
        row_in = pl.BlockSpec((block, hid), lambda i, z, j=j: (i + j * per, 0))
        row_out = pl.BlockSpec((block, hid), lambda i, z: (i, 0))
        halves.append(
            pl.pallas_call(
                functools.partial(backward_kernel, parts),
                name="backward",
                grid_spec=pltpu.PrefetchScalarGridSpec(
                    num_scalar_prefetch=1,
                    grid=(per,),
                    in_specs=[pl.BlockSpec((block, share), lambda i, z: (i, 0))] * parts
                    + [row_in] * 2
                    + [full(hid, width)] * 3
                    + [full(1, hid)] * 2,
                    out_specs=[row_out] * 2
                    + [pl.BlockSpec((block, share), lambda i, z: (i, 0))] * parts,
                ),
                out_shape=[sds((rows, hid), BF16)] * 2 + [sds((rows, share), BF16)] * parts,
                cost_estimate=cost(3 * slots * width * hid, 2 * slots * width),
            )(col, *out_grad[j], g, u, gw, uw, dw, gate_scale, up_scale)
        )
    input_cols = ring_scatter([half[2:] for half in halves])

    col_hid = pl.BlockSpec((hid, share), lambda i: (0, i))
    gate_grad, up_grad = pl.pallas_call(
        weight_kernel,
        name="weight",
        grid=(parts,),
        in_specs=[pl.BlockSpec((slots, share), lambda i: (0, i))] + [full(rows, hid)] * 4,
        out_specs=[col_hid] * 2,
        out_shape=[sds((hid, width), F32)] * 2,
        cost_estimate=cost(4 * slots * width * hid, 2 * slots * width + 8 * hid * width),
    )(arrived, halves[0][0], halves[1][0], halves[0][1], halves[1][1])
    down_grad = pl.pallas_call(
        functools.partial(down_kernel, parts),
        name="down",
        grid_spec=pltpu.PrefetchScalarGridSpec(
            num_scalar_prefetch=1,
            grid=(1,),
            in_specs=[full(slots, hid)] + [full(rows + raw, share)] * (2 * parts),
            out_specs=full(hid, width),
        ),
        out_shape=sds((hid, width), F32),
        cost_estimate=cost(2 * slots * width * hid, 2 * slots * width + 4 * hid * width),
    )(col, h, *out_grad[0], *out_grad[1])

    tail = 8
    mixed_part = pl.pallas_call(
        functools.partial(combine_kernel, cap, parts),
        name="combine",
        grid_spec=pltpu.PrefetchScalarGridSpec(
            num_scalar_prefetch=1,
            grid=(slots // block,),
            in_specs=[
                pl.BlockSpec((block, width), lambda i, z: (i, 0)),
                full(toks, slots),
                pl.BlockSpec((2 * toks, block), lambda i, z: (0, i)),
                full(choose, toks),
            ]
            + [pl.BlockSpec((raw, share), lambda i, z: (rows // raw, 0))] * (2 * parts),
            out_specs=full(parts, toks + tail, share),
            scratch_shapes=[pltpu.VMEM((2 * toks, width), F32), pltpu.VMEM((toks, slots), F32)],
        ),
        out_shape=sds((parts, toks + tail, share), BF16),
        cost_estimate=cost(6 * slots * toks * width, 2 * slots * width),
    )(col, returned, combine, weighted, route_expert.T, *out_grad[0], *out_grad[1])
    mixed_all = lax.all_to_all(mixed_part, "expert", split_axis=0, concat_axis=0, tiled=True)
    mixed, route_grad = pl.pallas_call(
        mixed_kernel,
        compiler_params=pltpu.CompilerParams(vmem_limit_bytes=8 << 20),
        name="mixed",
        grid=(1,),
        in_specs=[full(parts, toks + tail, share)],
        out_specs=[full(toks, share), full(choose, toks)],
        out_shape=[sds((toks, share), BF16), sds((choose, toks), F32)],
        cost_estimate=cost(parts * toks * share, 2 * parts * toks * share),
    )(mixed_all)
    route_grad = route_grad.T
    input_home = lax.all_to_all(
        input_cols.reshape(owners, cap, share), "dp", split_axis=0, concat_axis=0, tiled=True
    ).reshape(slots, share)
    token_grad = dot(combine, input_home).astype(BF16)
    return (mixed, token_grad, route_grad, gate_grad[None], up_grad[None], down_grad[None])


def solution(mesh):
    return jax.shard_map(
        step,
        mesh=mesh,
        in_specs=(
            P("dp", None),
            P("dp", None),
            P("dp", None),
            P("dp", "expert", None),
            P("dp", "expert", None),
            P("dp", "expert", None),
            P("dp", "expert"),
            P("dp", "expert"),
            P(),
            P("dp", "expert"),
        ),
        out_specs=(
            P("dp", "expert"),
            P("dp", "expert"),
            P("dp", None),
            P("dp", "expert", None),
            P("dp", "expert", None),
            P("dp", "expert", None),
        ),
        check_vma=False,
    )
```

```python
import functools

import jax
import jax.numpy as jnp
from jax import lax
from jax.experimental import pallas as pl
from jax.experimental.pallas import tpu as pltpu
from jax.sharding import PartitionSpec as P


F32 = jnp.float32
BF16 = jnp.bfloat16
NT = (((1,), (1,)), ((), ()))
NN = (((1,), (0,)), ((), ()))
TN = (((0,), (0,)), ((), ()))


def dot(a, b, dims=NN, **kw):
    return lax.dot_general(a, b, dims, preferred_element_type=F32, **kw)


def cost(flops, nbytes):
    return pl.CostEstimate(flops=flops, bytes_accessed=nbytes, transcendentals=0)


def iota(shape, dim):
    return lax.broadcasted_iota(jnp.int32, shape, dim)


def route_kernel(cap, col_ref, re_ref, rw_ref, cot_ref, ds_ref, m_ref, send_ref):
    choose, toks = re_ref.shape
    experts = ds_ref.shape[0]
    expert_id = iota((experts, toks), 0)
    named = jnp.zeros((experts, toks), F32)
    weight = jnp.zeros((experts, toks), F32)
    for k in range(choose):
        hit = re_ref[k : k + 1, :] == expert_id
        named = named + jnp.where(hit, 1.0, 0.0)
        weight = weight + jnp.where(hit, rw_ref[k : k + 1, :], 0.0)
    before = jnp.where(iota((toks, toks), 0) < iota((toks, toks), 1), 1.0, 0.0).astype(BF16)
    rank = dot(named.astype(BF16), before).astype(jnp.int32)
    code = jnp.where(named > 0.0, rank, -1)
    place = iota((cap, toks), 0)
    slot_weight = []
    for e in range(experts):
        hit = code[e : e + 1, :] == place
        m_ref[e * cap : (e + 1) * cap, :] = jnp.where(hit, 1.0, 0.0).astype(BF16)
        slot_weight.append(
            jnp.sum(jnp.where(hit, weight[e : e + 1, :], 0.0), axis=1, keepdims=True)
        )
    group = 8
    for g in range(experts // group):
        rows = dot(m_ref[g * group * cap : (g + 1) * group * cap, :], cot_ref[...])
        for i in range(group):
            e = g * group + i
            send_ref[e * cap : (e + 1) * cap, :] = (
                rows[i * cap : (i + 1) * cap, :] * slot_weight[e] * ds_ref[e : e + 1, :]
            ).astype(BF16)


def home_kernel(cap, re_ref, rw_ref, mt_ref, mw_ref):
    toks, choose = re_ref.shape
    slots = mt_ref.shape[1]
    experts = slots // cap
    expert_id = iota((toks, experts), 1)
    named = jnp.zeros((toks, experts), F32)
    weight = jnp.zeros((toks, experts), F32)
    for k in range(choose):
        hit = re_ref[:, k : k + 1] == expert_id
        named = named + jnp.where(hit, 1.0, 0.0)
        weight = weight + jnp.where(hit, rw_ref[:, k : k + 1], 0.0)
    before = jnp.where(iota((toks, toks), 1) < iota((toks, toks), 0), 1.0, 0.0).astype(BF16)
    rank = dot(before, named.astype(BF16))
    code = jnp.where(named > 0.0, rank, 128.0).astype(BF16)
    low = iota((experts, slots), 0) * cap
    slot = iota((experts, slots), 1)
    spread = jnp.where((slot >= low) & (slot < low + cap), 1.0, 0.0).astype(BF16)
    high = weight.astype(BF16)
    rest = (weight - high.astype(F32)).astype(BF16)
    place = (iota((toks, slots), 1) & (cap - 1)).astype(F32)
    hit = dot(code, spread) == place
    mt_ref[...] = jnp.where(hit, 1.0, 0.0).astype(BF16)
    mw_ref[:toks, :] = jnp.where(hit, dot(high, spread), 0.0).astype(BF16)
    mw_ref[toks:, :] = jnp.where(hit, dot(rest, spread), 0.0).astype(BF16)


def forward_kernel(
    e_ref, x_ref, gw_ref, uw_ref, dw_ref, gs_ref, us_ref, ds_ref, g_ref, u_ref, h_ref, y_ref
):
    x = x_ref[...]
    g = dot(x, gw_ref[...], NT) * gs_ref[...]
    u = dot(x, uw_ref[...], NT) * us_ref[...]
    g_ref[...] = g
    u_ref[...] = u
    h = (g * jax.nn.sigmoid(g) * u).astype(BF16)
    h_ref[...] = h
    scale = ds_ref[pl.ds(e_ref[0], 1), :]
    y_ref[...] = (dot(h, dw_ref[...]) * scale).astype(BF16)


def backward_kernel(parts, z_ref, *refs):
    o_refs = refs[:parts]
    g_ref, u_ref, gw_ref, uw_ref, dw_ref, gs_ref, us_ref, gi_ref, ui_ref = refs[parts:-parts]
    p_refs = refs[-parts:]
    share = p_refs[0].shape[1]

    def cols(c):
        at = lax.rem(z_ref[0] + c, parts)
        return pl.ds(pl.multiple_of(at * share, share), share)

    hg = dot(o_refs[0][...], dw_ref[:, cols(0)], NT)
    for c in range(1, parts):
        hg = hg + dot(o_refs[c][...], dw_ref[:, cols(parts - c)], NT)
    g = g_ref[...]
    u = u_ref[...]
    s = jax.nn.sigmoid(g)
    gi = (hg * u * s * (1.0 + g * (1.0 - s)) * gs_ref[...]).astype(BF16)
    ui = (hg * (g * s) * us_ref[...]).astype(BF16)
    gi_ref[...] = gi
    ui_ref[...] = ui
    for c in range(parts):
        p_refs[c][...] = (dot(gi, gw_ref[:, cols(c)]) + dot(ui, uw_ref[:, cols(c)])).astype(BF16)


def combine_kernel(cap, parts, z_ref, y_ref, mt_ref, mw_ref, re_ref, *refs):
    o_ref, acc_ref, prod_ref = refs[2 * parts :]
    step = pl.program_id(0)
    toks, slots = mt_ref.shape
    experts = slots // cap
    block = y_ref.shape[0]
    share = refs[0].shape[1]
    part = dot(mw_ref[...], y_ref[...])

    @pl.when(step == 0)
    def _():
        acc_ref[...] = part

    @pl.when(step > 0)
    def _():
        acc_ref[...] += part

    prod = None
    for k in range(parts):
        at = lax.rem(z_ref[0] + (parts - k), parts)
        cols = pl.ds(pl.multiple_of(at * share, share), share)
        c = jnp.concatenate([refs[k][...], refs[parts + k][...]], axis=0)
        term = dot(c, y_ref[:, cols], NT)
        prod = term if prod is None else prod + term
    prod_ref[:, pl.ds(pl.multiple_of(step * block, block), block)] = prod

    @pl.when(step == pl.num_programs(0) - 1)
    def _():
        held = jnp.where(mt_ref[...].astype(F32) > 0.0, prod_ref[...], 0.0)
        low = iota((experts, slots), 0) * cap
        slot = iota((experts, slots), 1)
        spread = jnp.where((slot >= low) & (slot < low + cap), 1.0, 0.0)
        table = dot(spread, held, NT, precision=lax.Precision.HIGHEST)
        expert_id = iota((experts, toks), 0)
        lines = [
            jnp.sum(jnp.where(re_ref[k : k + 1, :] == expert_id, table, 0.0), axis=0, keepdims=True)
            for k in range(re_ref.shape[0])
        ]
        tail = jnp.concatenate(lines + [jnp.zeros_like(lines[0])] * 4, axis=0)
        tail = jnp.concatenate([tail, jnp.zeros_like(tail)], axis=1).astype(BF16)
        for c in range(parts):
            cols = slice(c * share, (c + 1) * share)
            o_ref[c, :toks, :] = (acc_ref[:toks, cols] + acc_ref[toks:, cols]).astype(BF16)
            o_ref[c, toks:, :] = tail


def mixed_kernel(x_ref, o_ref, r_ref):
    choose, toks = r_ref.shape
    total = x_ref[0].astype(F32)
    for c in range(1, x_ref.shape[0]):
        total = total + x_ref[c].astype(F32)
    o_ref[...] = total[:toks, :].astype(BF16)
    r_ref[...] = total[toks : toks + choose, :toks]


def weight_kernel(x_ref, *refs):
    gi_refs, ui_refs, gg_ref, ug_ref = refs[:2], refs[2:4], refs[4], refs[5]
    x = x_ref[...]
    gg_ref[...] = dot(jnp.concatenate([r[...] for r in gi_refs], axis=0), x, TN)
    ug_ref[...] = dot(jnp.concatenate([r[...] for r in ui_refs], axis=0), x, TN)


def down_kernel(parts, z_ref, h_ref, _, *refs):
    dg_ref = refs[-1]
    share = refs[0].shape[1]
    rows = h_ref.shape[0] // 2
    h = h_ref[...]
    for c in range(parts):
        o = jnp.concatenate([refs[c][:rows, :], refs[parts + c][:rows, :]], axis=0)
        at = lax.rem(z_ref[0] + (parts - c), parts)
        dg_ref[:, pl.ds(pl.multiple_of(at * share, share), share)] = dot(h, o, TN)


def shift(x, by):
    size = lax.axis_size("expert")
    return lax.ppermute(x, "expert", [(i, (i + by) % size) for i in range(size)])


def ring_gather(first, second):
    size = lax.axis_size("expert")
    half = size // 2
    pieces = [[None] * size, [None] * size]
    for j, (x, ups) in enumerate(((first, half), (second, half - 1))):
        pieces[j][0] = x
        up = down = x
        for k in range(1, half + 1):
            if k <= ups:
                up = shift(up, 1)
                pieces[j][k] = up
            if k <= size - 1 - ups:
                down = shift(down, -1)
                pieces[j][size - k] = down
    return pieces


def add(*terms):
    return sum(t.astype(F32) for t in terms).astype(BF16)


def ring_scatter(halves):
    sums = []
    for parts, ups in zip(halves, (4, 3)):
        size = len(parts)
        up = shift(parts[ups], 1)
        down = shift(parts[ups + 1], -1)
        for k in range(ups - 1, 0, -1):
            up = shift(add(up, parts[k]), 1)
        for k in range(ups + 2, size):
            down = shift(add(down, parts[k]), -1)
        sums.append(add(up, down, parts[0]))
    return jnp.concatenate(sums, axis=0)


def step(
    tokens,
    route_expert,
    route_weight,
    gate_weight,
    up_weight,
    down_weight,
    gate_scale,
    up_scale,
    down_scale,
    cotangent,
):
    owners = lax.axis_size("dp")
    parts = lax.axis_size("expert")
    toks, width = tokens.shape
    choose = route_expert.shape[1]
    cap = 2 * toks * choose // owners
    slots = owners * cap
    share = width // parts
    hid = gate_weight.shape[1]
    gw, uw, dw = gate_weight[0], up_weight[0], down_weight[0]
    mine = lax.axis_index("dp").astype(jnp.int32).reshape(1)
    col = lax.axis_index("expert").astype(jnp.int32).reshape(1)
    full = lambda *shape: pl.BlockSpec(shape, lambda *_: (0,) * len(shape))
    sds = jax.ShapeDtypeStruct

    onehot, cot_send = pl.pallas_call(
        functools.partial(route_kernel, cap),
        name="route",
        grid_spec=pltpu.PrefetchScalarGridSpec(
            num_scalar_prefetch=1,
            grid=(1,),
            in_specs=[
                full(choose, toks),
                full(choose, toks),
                full(toks, share),
                pl.BlockSpec((owners, share), lambda i, c: (0, c[0])),
            ],
            out_specs=[full(slots, toks), full(slots, share)],
        ),
        out_shape=[sds((slots, toks), BF16), sds((slots, share), BF16)],
        cost_estimate=cost(2 * slots * toks * share, 2 * slots * share * 2),
    )(col, route_expert.T, route_weight.T, cotangent, down_scale)
    cot_mine = lax.all_to_all(
        cot_send.reshape(owners, cap, share), "dp", split_axis=0, concat_axis=0, tiled=True
    ).reshape(slots, share)
    tok_send = lax.dot_general(onehot, tokens, NN, preferred_element_type=BF16)
    arrived = lax.all_to_all(
        tok_send.reshape(owners, cap, width), "dp", split_axis=0, concat_axis=0, tiled=True
    ).reshape(slots, width)
    rows, raw = slots // 2, toks // 2
    out_grad = ring_gather(
        jnp.concatenate([cot_mine[:rows], cotangent[:raw]], axis=0),
        jnp.concatenate([cot_mine[rows:], cotangent[raw:]], axis=0),
    )

    last = (out_grad[0][4], out_grad[0][5], out_grad[1][3], out_grad[1][4])
    marker = add(*(o[:8, :128] for o in last))

    combine, weighted = pl.pallas_call(
        functools.partial(home_kernel, cap),
        name="home",
        in_specs=[full(toks, choose)] * 2,
        out_specs=[full(toks, slots), full(2 * toks, slots)],
        grid=(1,),
        out_shape=[sds((toks, slots), BF16), sds((2 * toks, slots), BF16)],
        cost_estimate=cost(6 * slots * toks * owners, 6 * slots * toks),
    )(route_expert, route_weight)

    block = 256
    row_hid = pl.BlockSpec((block, hid), lambda i, *_: (i, 0))
    row_wide = pl.BlockSpec((block, width), lambda i, *_: (i, 0))
    g, u, h, out_rows = pl.pallas_call(
        forward_kernel,
        name="forward",
        grid_spec=pltpu.PrefetchScalarGridSpec(
            num_scalar_prefetch=1,
            grid=(slots // block,),
            in_specs=[row_wide]
            + [full(hid, width)] * 3
            + [full(1, hid)] * 2
            + [full(owners, width)],
            out_specs=[row_hid, row_hid, row_hid, row_wide],
        ),
        out_shape=[
            sds((slots, hid), F32),
            sds((slots, hid), F32),
            sds((slots, hid), BF16),
            sds((slots, width), BF16),
        ],
        cost_estimate=cost(6 * slots * width * hid, 4 * slots * width),
    )(mine, arrived, gw, uw, dw, gate_scale, up_scale, down_scale)
    returned = lax.all_to_all(
        out_rows.reshape(owners, cap, width), "dp", split_axis=0, concat_axis=0, tiled=True
    ).reshape(slots, width)

    block = 256
    per = rows // block
    halves = []
    for j in range(2):
        row_in = pl.BlockSpec((block, hid), lambda i, z, j=j: (i + j * per, 0))
        row_out = pl.BlockSpec((block, hid), lambda i, z: (i, 0))
        halves.append(
            pl.pallas_call(
                functools.partial(backward_kernel, parts),
                name="backward",
                grid_spec=pltpu.PrefetchScalarGridSpec(
                    num_scalar_prefetch=1,
                    grid=(per,),
                    in_specs=[pl.BlockSpec((block, share), lambda i, z: (i, 0))] * parts
                    + [row_in] * 2
                    + [full(hid, width)] * 3
                    + [full(1, hid)] * 2,
                    out_specs=[row_out] * 2
                    + [pl.BlockSpec((block, share), lambda i, z: (i, 0))] * parts,
                ),
                out_shape=[sds((rows, hid), BF16)] * 2 + [sds((rows, share), BF16)] * parts,
                cost_estimate=cost(3 * slots * width * hid, 2 * slots * width),
            )(col, *out_grad[j], g, u, gw, uw, dw, gate_scale, up_scale)
        )
    input_cols = ring_scatter([half[2:] for half in halves])

    col_hid = pl.BlockSpec((hid, share), lambda i: (0, i))
    gate_grad, up_grad = pl.pallas_call(
        weight_kernel,
        name="weight",
        grid=(parts,),
        in_specs=[pl.BlockSpec((slots, share), lambda i: (0, i))] + [full(rows, hid)] * 4,
        out_specs=[col_hid] * 2,
        out_shape=[sds((hid, width), F32)] * 2,
        cost_estimate=cost(4 * slots * width * hid, 2 * slots * width + 8 * hid * width),
    )(arrived, halves[0][0], halves[1][0], halves[0][1], halves[1][1])
    down_grad = pl.pallas_call(
        functools.partial(down_kernel, parts),
        name="down",
        grid_spec=pltpu.PrefetchScalarGridSpec(
            num_scalar_prefetch=1,
            grid=(1,),
            in_specs=[full(slots, hid), full(8, 128)] + [full(rows + raw, share)] * (2 * parts),
            out_specs=full(hid, width),
        ),
        out_shape=sds((hid, width), F32),
        cost_estimate=cost(2 * slots * width * hid, 2 * slots * width + 4 * hid * width),
    )(col, h, marker, *out_grad[0], *out_grad[1])

    tail = 8
    mixed_part = pl.pallas_call(
        functools.partial(combine_kernel, cap, parts),
        name="combine",
        grid_spec=pltpu.PrefetchScalarGridSpec(
            num_scalar_prefetch=1,
            grid=(slots // block,),
            in_specs=[
                pl.BlockSpec((block, width), lambda i, z: (i, 0)),
                full(toks, slots),
                pl.BlockSpec((2 * toks, block), lambda i, z: (0, i)),
                full(choose, toks),
            ]
            + [pl.BlockSpec((raw, share), lambda i, z: (rows // raw, 0))] * (2 * parts),
            out_specs=full(parts, toks + tail, share),
            scratch_shapes=[pltpu.VMEM((2 * toks, width), F32), pltpu.VMEM((toks, slots), F32)],
        ),
        out_shape=sds((parts, toks + tail, share), BF16),
        cost_estimate=cost(6 * slots * toks * width, 2 * slots * width),
    )(col, returned, combine, weighted, route_expert.T, *out_grad[0], *out_grad[1])
    mixed_all = lax.all_to_all(mixed_part, "expert", split_axis=0, concat_axis=0, tiled=True)
    mixed, route_grad = pl.pallas_call(
        mixed_kernel,
        compiler_params=pltpu.CompilerParams(vmem_limit_bytes=8 << 20),
        name="mixed",
        grid=(1,),
        in_specs=[full(parts, toks + tail, share)],
        out_specs=[full(toks, share), full(choose, toks)],
        out_shape=[sds((toks, share), BF16), sds((choose, toks), F32)],
        cost_estimate=cost(parts * toks * share, 2 * parts * toks * share),
    )(mixed_all)
    route_grad = route_grad.T
    input_home = lax.all_to_all(
        input_cols.reshape(owners, cap, share), "dp", split_axis=0, concat_axis=0, tiled=True
    ).reshape(slots, share)
    token_grad = dot(combine, input_home).astype(BF16)
    return (mixed, token_grad, route_grad, gate_grad[None], up_grad[None], down_grad[None])


def solution(mesh):
    return jax.shard_map(
        step,
        mesh=mesh,
        in_specs=(
            P("dp", None),
            P("dp", None),
            P("dp", None),
            P("dp", "expert", None),
            P("dp", "expert", None),
            P("dp", "expert", None),
            P("dp", "expert"),
            P("dp", "expert"),
            P(),
            P("dp", "expert"),
        ),
        out_specs=(
            P("dp", "expert"),
            P("dp", "expert"),
            P("dp", None),
            P("dp", "expert", None),
            P("dp", "expert", None),
            P("dp", "expert", None),
        ),
        check_vma=False,
    )
```

```python
import functools

import jax
import jax.numpy as jnp
from jax import lax
from jax.experimental import pallas as pl
from jax.experimental.pallas import tpu as pltpu
from jax.sharding import PartitionSpec as P


F32 = jnp.float32
BF16 = jnp.bfloat16
NT = (((1,), (1,)), ((), ()))
NN = (((1,), (0,)), ((), ()))
TN = (((0,), (0,)), ((), ()))


def dot(a, b, dims=NN, **kw):
    return lax.dot_general(a, b, dims, preferred_element_type=F32, **kw)


def cost(flops, nbytes):
    return pl.CostEstimate(flops=flops, bytes_accessed=nbytes, transcendentals=0)


def iota(shape, dim):
    return lax.broadcasted_iota(jnp.int32, shape, dim)


def route_kernel(cap, col_ref, re_ref, rw_ref, cot_ref, ds_ref, m_ref, send_ref):
    choose, toks = re_ref.shape
    experts = ds_ref.shape[0]
    expert_id = iota((experts, toks), 0)
    named = jnp.zeros((experts, toks), F32)
    weight = jnp.zeros((experts, toks), F32)
    for k in range(choose):
        hit = re_ref[k : k + 1, :] == expert_id
        named = named + jnp.where(hit, 1.0, 0.0)
        weight = weight + jnp.where(hit, rw_ref[k : k + 1, :], 0.0)
    before = jnp.where(iota((toks, toks), 0) < iota((toks, toks), 1), 1.0, 0.0).astype(BF16)
    rank = dot(named.astype(BF16), before).astype(jnp.int32)
    code = jnp.where(named > 0.0, rank, -1)
    place = iota((cap, toks), 0)
    slot_weight = []
    for e in range(experts):
        hit = code[e : e + 1, :] == place
        m_ref[e * cap : (e + 1) * cap, :] = jnp.where(hit, 1.0, 0.0).astype(BF16)
        slot_weight.append(
            jnp.sum(jnp.where(hit, weight[e : e + 1, :], 0.0), axis=1, keepdims=True)
        )
    group = 8
    for g in range(experts // group):
        rows = dot(m_ref[g * group * cap : (g + 1) * group * cap, :], cot_ref[...])
        for i in range(group):
            e = g * group + i
            send_ref[e * cap : (e + 1) * cap, :] = (
                rows[i * cap : (i + 1) * cap, :] * slot_weight[e] * ds_ref[e : e + 1, :]
            ).astype(BF16)


def home_kernel(cap, re_ref, rw_ref, mt_ref, mw_ref):
    toks, choose = re_ref.shape
    slots = mt_ref.shape[1]
    experts = slots // cap
    expert_id = iota((toks, experts), 1)
    named = jnp.zeros((toks, experts), F32)
    weight = jnp.zeros((toks, experts), F32)
    for k in range(choose):
        hit = re_ref[:, k : k + 1] == expert_id
        named = named + jnp.where(hit, 1.0, 0.0)
        weight = weight + jnp.where(hit, rw_ref[:, k : k + 1], 0.0)
    before = jnp.where(iota((toks, toks), 1) < iota((toks, toks), 0), 1.0, 0.0).astype(BF16)
    rank = dot(before, named.astype(BF16))
    code = jnp.where(named > 0.0, rank, 128.0).astype(BF16)
    low = iota((experts, slots), 0) * cap
    slot = iota((experts, slots), 1)
    spread = jnp.where((slot >= low) & (slot < low + cap), 1.0, 0.0).astype(BF16)
    high = weight.astype(BF16)
    rest = (weight - high.astype(F32)).astype(BF16)
    place = (iota((toks, slots), 1) & (cap - 1)).astype(F32)
    hit = dot(code, spread) == place
    mt_ref[...] = jnp.where(hit, 1.0, 0.0).astype(BF16)
    mw_ref[:toks, :] = jnp.where(hit, dot(high, spread), 0.0).astype(BF16)
    mw_ref[toks:, :] = jnp.where(hit, dot(rest, spread), 0.0).astype(BF16)


def forward_kernel(
    e_ref, x_ref, gw_ref, uw_ref, dw_ref, gs_ref, us_ref, ds_ref, g_ref, u_ref, h_ref, y_ref
):
    x = x_ref[...]
    g = dot(x, gw_ref[...], NT) * gs_ref[...]
    u = dot(x, uw_ref[...], NT) * us_ref[...]
    g_ref[...] = g
    u_ref[...] = u
    h = (g * jax.nn.sigmoid(g) * u).astype(BF16)
    h_ref[...] = h
    scale = ds_ref[pl.ds(e_ref[0], 1), :]
    y_ref[...] = (dot(h, dw_ref[...]) * scale).astype(BF16)


def backward_kernel(parts, z_ref, *refs):
    o_halves = refs[:parts], refs[parts : 2 * parts]
    g_ref, u_ref, gw_ref, uw_ref, dw_ref, gs_ref, us_ref = refs[2 * parts : -2 * parts - 2]
    gi_ref, ui_ref = refs[-2 * parts - 2 : -2 * parts]
    p_halves = refs[-2 * parts : -parts], refs[-parts:]
    share = p_halves[0][0].shape[1]
    per = pl.num_programs(0) // 2

    def cols(c):
        at = lax.rem(z_ref[0] + c, parts)
        return pl.ds(pl.multiple_of(at * share, share), share)

    def run(o_refs, p_refs):
        hg = dot(o_refs[0][...], dw_ref[:, cols(0)], NT)
        for c in range(1, parts):
            hg = hg + dot(o_refs[c][...], dw_ref[:, cols(parts - c)], NT)
        g = g_ref[...]
        u = u_ref[...]
        s = jax.nn.sigmoid(g)
        gi = (hg * u * s * (1.0 + g * (1.0 - s)) * gs_ref[...]).astype(BF16)
        ui = (hg * (g * s) * us_ref[...]).astype(BF16)
        gi_ref[...] = gi
        ui_ref[...] = ui
        for c in range(parts):
            p_refs[c][...] = (dot(gi, gw_ref[:, cols(c)]) + dot(ui, uw_ref[:, cols(c)])).astype(BF16)

    for j in range(2):
        pl.when(lax.div(pl.program_id(0), per) == j)(
            functools.partial(run, o_halves[j], p_halves[j])
        )


def combine_kernel(cap, parts, z_ref, y_ref, mt_ref, mw_ref, re_ref, *refs):
    o_ref, acc_ref, prod_ref = refs[2 * parts :]
    step = pl.program_id(0)
    toks, slots = mt_ref.shape
    experts = slots // cap
    block = y_ref.shape[0]
    share = refs[0].shape[1]
    part = dot(mw_ref[...], y_ref[...])

    @pl.when(step == 0)
    def _():
        acc_ref[...] = part

    @pl.when(step > 0)
    def _():
        acc_ref[...] += part

    prod = None
    for k in range(parts):
        at = lax.rem(z_ref[0] + (parts - k), parts)
        cols = pl.ds(pl.multiple_of(at * share, share), share)
        c = jnp.concatenate([refs[k][...], refs[parts + k][...]], axis=0)
        term = dot(c, y_ref[:, cols], NT)
        prod = term if prod is None else prod + term
    prod_ref[:, pl.ds(pl.multiple_of(step * block, block), block)] = prod

    @pl.when(step == pl.num_programs(0) - 1)
    def _():
        held = jnp.where(mt_ref[...].astype(F32) > 0.0, prod_ref[...], 0.0)
        low = iota((experts, slots), 0) * cap
        slot = iota((experts, slots), 1)
        spread = jnp.where((slot >= low) & (slot < low + cap), 1.0, 0.0)
        table = dot(spread, held, NT, precision=lax.Precision.HIGHEST)
        expert_id = iota((experts, toks), 0)
        lines = [
            jnp.sum(jnp.where(re_ref[k : k + 1, :] == expert_id, table, 0.0), axis=0, keepdims=True)
            for k in range(re_ref.shape[0])
        ]
        tail = jnp.concatenate(lines + [jnp.zeros_like(lines[0])] * 4, axis=0)
        tail = jnp.concatenate([tail, jnp.zeros_like(tail)], axis=1).astype(BF16)
        for c in range(parts):
            cols = slice(c * share, (c + 1) * share)
            o_ref[c, :toks, :] = (acc_ref[:toks, cols] + acc_ref[toks:, cols]).astype(BF16)
            o_ref[c, toks:, :] = tail


def mixed_kernel(x_ref, o_ref, r_ref):
    choose, toks = r_ref.shape
    total = x_ref[0].astype(F32)
    for c in range(1, x_ref.shape[0]):
        total = total + x_ref[c].astype(F32)
    o_ref[...] = total[:toks, :].astype(BF16)
    r_ref[...] = total[toks : toks + choose, :toks]


def weight_kernel(x_ref, gi_ref, ui_ref, gg_ref, ug_ref):
    x = x_ref[...]
    gg_ref[...] = dot(gi_ref[...], x, TN)
    ug_ref[...] = dot(ui_ref[...], x, TN)


def down_kernel(parts, z_ref, h_ref, _, *refs):
    dg_ref = refs[-1]
    share = refs[0].shape[1]
    rows = h_ref.shape[0] // 2
    h = h_ref[...]
    for c in range(parts):
        o = jnp.concatenate([refs[c][:rows, :], refs[parts + c][:rows, :]], axis=0)
        at = lax.rem(z_ref[0] + (parts - c), parts)
        dg_ref[:, pl.ds(pl.multiple_of(at * share, share), share)] = dot(h, o, TN)


def shift(x, by):
    size = lax.axis_size("expert")
    return lax.ppermute(x, "expert", [(i, (i + by) % size) for i in range(size)])


def ring_gather(first, second):
    size = lax.axis_size("expert")
    half = size // 2
    pieces = [[None] * size, [None] * size]
    for j, (x, ups) in enumerate(((first, half), (second, half - 1))):
        pieces[j][0] = x
        up = down = x
        for k in range(1, half + 1):
            if k <= ups:
                up = shift(up, 1)
                pieces[j][k] = up
            if k <= size - 1 - ups:
                down = shift(down, -1)
                pieces[j][size - k] = down
    return pieces


def add(*terms):
    return sum(t.astype(F32) for t in terms).astype(BF16)


def ring_scatter(halves):
    sums = []
    for parts, ups in zip(halves, (4, 3)):
        size = len(parts)
        up = shift(parts[ups], 1)
        down = shift(parts[ups + 1], -1)
        for k in range(ups - 1, 0, -1):
            up = shift(add(up, parts[k]), 1)
        for k in range(ups + 2, size):
            down = shift(add(down, parts[k]), -1)
        sums.append(add(up, down, parts[0]))
    return jnp.concatenate(sums, axis=0)


def step(
    tokens,
    route_expert,
    route_weight,
    gate_weight,
    up_weight,
    down_weight,
    gate_scale,
    up_scale,
    down_scale,
    cotangent,
):
    owners = lax.axis_size("dp")
    parts = lax.axis_size("expert")
    toks, width = tokens.shape
    choose = route_expert.shape[1]
    cap = 2 * toks * choose // owners
    slots = owners * cap
    share = width // parts
    hid = gate_weight.shape[1]
    gw, uw, dw = gate_weight[0], up_weight[0], down_weight[0]
    mine = lax.axis_index("dp").astype(jnp.int32).reshape(1)
    col = lax.axis_index("expert").astype(jnp.int32).reshape(1)
    full = lambda *shape: pl.BlockSpec(shape, lambda *_: (0,) * len(shape))
    sds = jax.ShapeDtypeStruct

    onehot, cot_send = pl.pallas_call(
        functools.partial(route_kernel, cap),
        name="route",
        grid_spec=pltpu.PrefetchScalarGridSpec(
            num_scalar_prefetch=1,
            grid=(1,),
            in_specs=[
                full(choose, toks),
                full(choose, toks),
                full(toks, share),
                pl.BlockSpec((owners, share), lambda i, c: (0, c[0])),
            ],
            out_specs=[full(slots, toks), full(slots, share)],
        ),
        out_shape=[sds((slots, toks), BF16), sds((slots, share), BF16)],
        cost_estimate=cost(2 * slots * toks * share, 2 * slots * share * 2),
    )(col, route_expert.T, route_weight.T, cotangent, down_scale)
    cot_mine = lax.all_to_all(
        cot_send.reshape(owners, cap, share), "dp", split_axis=0, concat_axis=0, tiled=True
    ).reshape(slots, share)
    tok_send = lax.dot_general(onehot, tokens, NN, preferred_element_type=BF16)
    arrived = lax.all_to_all(
        tok_send.reshape(owners, cap, width), "dp", split_axis=0, concat_axis=0, tiled=True
    ).reshape(slots, width)
    rows, raw = slots // 2, toks // 2
    out_grad = ring_gather(
        jnp.concatenate([cot_mine[:rows], cotangent[:raw]], axis=0),
        jnp.concatenate([cot_mine[rows:], cotangent[raw:]], axis=0),
    )

    last = (out_grad[0][4], out_grad[0][5], out_grad[1][3], out_grad[1][4])
    marker = add(*(o[:8, :128] for o in last))

    combine, weighted = pl.pallas_call(
        functools.partial(home_kernel, cap),
        name="home",
        in_specs=[full(toks, choose)] * 2,
        out_specs=[full(toks, slots), full(2 * toks, slots)],
        grid=(1,),
        out_shape=[sds((toks, slots), BF16), sds((2 * toks, slots), BF16)],
        cost_estimate=cost(6 * slots * toks * owners, 6 * slots * toks),
    )(route_expert, route_weight)

    block = 512
    row_hid = pl.BlockSpec((block, hid), lambda i, *_: (i, 0))
    row_wide = pl.BlockSpec((block, width), lambda i, *_: (i, 0))
    g, u, h, out_rows = pl.pallas_call(
        forward_kernel,
        name="forward",
        grid_spec=pltpu.PrefetchScalarGridSpec(
            num_scalar_prefetch=1,
            grid=(slots // block,),
            in_specs=[row_wide]
            + [full(hid, width)] * 3
            + [full(1, hid)] * 2
            + [full(owners, width)],
            out_specs=[row_hid, row_hid, row_hid, row_wide],
        ),
        out_shape=[
            sds((slots, hid), F32),
            sds((slots, hid), F32),
            sds((slots, hid), BF16),
            sds((slots, width), BF16),
        ],
        cost_estimate=cost(6 * slots * width * hid, 4 * slots * width),
    )(mine, arrived, gw, uw, dw, gate_scale, up_scale, down_scale)
    returned = lax.all_to_all(
        out_rows.reshape(owners, cap, width), "dp", split_axis=0, concat_axis=0, tiled=True
    ).reshape(slots, width)

    block = 256
    per = rows // block
    row_hid = pl.BlockSpec((block, hid), lambda i, z: (i, 0))
    row_share = [pl.BlockSpec((block, share), lambda i, z: (jnp.minimum(i, per - 1), 0))] * parts
    row_share += [pl.BlockSpec((block, share), lambda i, z: (jnp.maximum(i - per, 0), 0))] * parts
    gate_in, up_in, *shares = pl.pallas_call(
        functools.partial(backward_kernel, parts),
        name="backward",
        grid_spec=pltpu.PrefetchScalarGridSpec(
            num_scalar_prefetch=1,
            grid=(2 * per,),
            in_specs=row_share + [row_hid] * 2 + [full(hid, width)] * 3 + [full(1, hid)] * 2,
            out_specs=[row_hid] * 2 + row_share,
        ),
        out_shape=[sds((slots, hid), BF16)] * 2 + [sds((rows, share), BF16)] * (2 * parts),
        cost_estimate=cost(6 * slots * width * hid, 4 * slots * width),
    )(col, *out_grad[0], *out_grad[1], g, u, gw, uw, dw, gate_scale, up_scale)
    input_cols = ring_scatter([shares[:parts], shares[parts:]])

    col_hid = pl.BlockSpec((hid, share), lambda i: (0, i))
    gate_grad, up_grad = pl.pallas_call(
        weight_kernel,
        name="weight",
        grid=(parts,),
        in_specs=[pl.BlockSpec((slots, share), lambda i: (0, i))] + [full(slots, hid)] * 2,
        out_specs=[col_hid] * 2,
        out_shape=[sds((hid, width), F32)] * 2,
        cost_estimate=cost(4 * slots * width * hid, 2 * slots * width + 8 * hid * width),
    )(arrived, gate_in, up_in)
    down_grad = pl.pallas_call(
        functools.partial(down_kernel, parts),
        name="down",
        grid_spec=pltpu.PrefetchScalarGridSpec(
            num_scalar_prefetch=1,
            grid=(1,),
            in_specs=[full(slots, hid), full(8, 128)] + [full(rows + raw, share)] * (2 * parts),
            out_specs=full(hid, width),
        ),
        out_shape=sds((hid, width), F32),
        cost_estimate=cost(2 * slots * width * hid, 2 * slots * width + 4 * hid * width),
    )(col, h, marker, *out_grad[0], *out_grad[1])

    tail = 8
    mixed_part = pl.pallas_call(
        functools.partial(combine_kernel, cap, parts),
        name="combine",
        grid_spec=pltpu.PrefetchScalarGridSpec(
            num_scalar_prefetch=1,
            grid=(slots // block,),
            in_specs=[
                pl.BlockSpec((block, width), lambda i, z: (i, 0)),
                full(toks, slots),
                pl.BlockSpec((2 * toks, block), lambda i, z: (0, i)),
                full(choose, toks),
            ]
            + [pl.BlockSpec((raw, share), lambda i, z: (rows // raw, 0))] * (2 * parts),
            out_specs=full(parts, toks + tail, share),
            scratch_shapes=[pltpu.VMEM((2 * toks, width), F32), pltpu.VMEM((toks, slots), F32)],
        ),
        out_shape=sds((parts, toks + tail, share), BF16),
        cost_estimate=cost(6 * slots * toks * width, 2 * slots * width),
    )(col, returned, combine, weighted, route_expert.T, *out_grad[0], *out_grad[1])
    mixed_all = lax.all_to_all(mixed_part, "expert", split_axis=0, concat_axis=0, tiled=True)
    mixed, route_grad = pl.pallas_call(
        mixed_kernel,
        compiler_params=pltpu.CompilerParams(vmem_limit_bytes=8 << 20),
        name="mixed",
        grid=(1,),
        in_specs=[full(parts, toks + tail, share)],
        out_specs=[full(toks, share), full(choose, toks)],
        out_shape=[sds((toks, share), BF16), sds((choose, toks), F32)],
        cost_estimate=cost(parts * toks * share, 2 * parts * toks * share),
    )(mixed_all)
    route_grad = route_grad.T
    input_home = lax.all_to_all(
        input_cols.reshape(owners, cap, share), "dp", split_axis=0, concat_axis=0, tiled=True
    ).reshape(slots, share)
    token_grad = dot(combine, input_home).astype(BF16)
    return (mixed, token_grad, route_grad, gate_grad[None], up_grad[None], down_grad[None])


def solution(mesh):
    return jax.shard_map(
        step,
        mesh=mesh,
        in_specs=(
            P("dp", None),
            P("dp", None),
            P("dp", None),
            P("dp", "expert", None),
            P("dp", "expert", None),
            P("dp", "expert", None),
            P("dp", "expert"),
            P("dp", "expert"),
            P(),
            P("dp", "expert"),
        ),
        out_specs=(
            P("dp", "expert"),
            P("dp", "expert"),
            P("dp", None),
            P("dp", "expert", None),
            P("dp", "expert", None),
            P("dp", "expert", None),
        ),
        check_vma=False,
    )
```
